32 devices in a mesh: row: 4 (over z), col: 8 (over y, x, core).
Axes of the slice: x: 2, y: 2, z: 4, core: 2. Of those that a mesh axis runs over, the one named last changes fastest.
Arguments:
- rho_real: float32 [4, 8, 1280000], P('row', 'col'), as said below
- rho_imag: float32 [4, 8, 1280000], P('row', 'col'), as said below
- cav_real: float32 [100, 100], replicated, may hold values from -0.4375 to 0.4375
- cav_imag: float32 [100, 100], replicated, may hold values from -0.4375 to 0.4375
- mech_real: float32 [64, 64], replicated, may hold values from -0.5 to 0.5
- mech_imag: float32 [64, 64], replicated, may hold values from -0.5 to 0.5
Outputs:
- out_real: float32 [4, 8, 1280000], P('row', 'col')
- out_imag: float32 [4, 8, 1280000], P('row', 'col')
The draws below stay inside these ranges and needn't reach their ends.
Inputs may be any that keep to these rules, and one draw needn't show every extreme that they name: rho_real is the real part of a Hermitian matrix: symmetric in the whole matrix's row and column index. rho_imag is the imaginary part of a Hermitian matrix: antisymmetric in the whole matrix's row and column index.
All inputs are finite; a program needn't handle non-finite values.
Results may differ from the reference program's by a relative error of at most 0.0001.
Values sent between devices are 32-bit elements; how exact they have to be, the bound alone decides.
No kernel may reach another device: no remote copies, remote signals or barrier semaphores. Data moves between devices by JAX's collectives and lax.ppermute only.
A program may use at most 192 MiB of HBM per device.

```python
import jax
import jax.numpy as jnp
from jax import lax

CAV = 100
MECH = 64
STEPS = 1
N_ROW = 4
N_COL = 8


def hermitian_part(key, salt, sign):
    order = CAV * MECH
    inner = jax.random.fold_in(key, salt)
    whole = jax.random.normal(inner, (order, order), jnp.float32)
    half = 0.5 * (whole + sign * jnp.transpose(whole))
    local_rows = MECH // N_ROW
    local_cols = MECH // N_COL
    shaped = half.reshape(N_ROW, local_rows, CAV, N_COL, local_cols, CAV)
    return jnp.transpose(shaped, (0, 3, 1, 2, 4, 5)).reshape(N_ROW, N_COL, local_rows * CAV * local_cols * CAV)


def draw_rho_real(key, part):
    return hermitian_part(key, 11, 1.0)


def draw_rho_imag(key, part):
    return hermitian_part(key, 23, -1.0)


def scatter_about(key, extent, spread, reach, dtype=jnp.bfloat16):
    values = jax.random.normal(key, extent, jnp.float32) * spread
    return jnp.minimum(jnp.maximum(values, -reach), reach).astype(dtype)


def setup_inputs(seed: int = 0) -> dict:
    keys = jax.random.split(jax.random.key(seed), 7)
    return {
        "rho_real": draw_rho_real(jax.random.fold_in(keys[6], 71), 0),
        "rho_imag": draw_rho_imag(jax.random.fold_in(keys[6], 71), 0),
        "cav_real": scatter_about(keys[2], (CAV, CAV), (2 * CAV) ** -0.5, 0.4375, jnp.float32),
        "cav_imag": scatter_about(keys[3], (CAV, CAV), (2 * CAV) ** -0.5, 0.4375, jnp.float32),
        "mech_real": scatter_about(keys[4], (MECH, MECH), (2 * MECH) ** -0.5, 0.5, jnp.float32),
        "mech_imag": scatter_about(keys[5], (MECH, MECH), (2 * MECH) ** -0.5, 0.5, jnp.float32),
    }


highest = lax.Precision.HIGHEST


def cavity_sides(real_part, imag_part, cav_real, cav_imag):
    left_real = jnp.einsum("cd,mdne->mcne", cav_real, real_part, precision=highest) - jnp.einsum("cd,mdne->mcne", cav_imag, imag_part, precision=highest)
    left_imag = jnp.einsum("cd,mdne->mcne", cav_real, imag_part, precision=highest) + jnp.einsum("cd,mdne->mcne", cav_imag, real_part, precision=highest)
    right_real = jnp.einsum("mcne,fe->mcnf", left_real, cav_real, precision=highest) + jnp.einsum("mcne,fe->mcnf", left_imag, cav_imag, precision=highest)
    right_imag = jnp.einsum("mcne,fe->mcnf", left_imag, cav_real, precision=highest) - jnp.einsum("mcne,fe->mcnf", left_real, cav_imag, precision=highest)
    return right_real, right_imag


def mech_kets(real_part, imag_part, mech_real, mech_imag):
    new_real = jnp.einsum("mn,ncqd->mcqd", mech_real, real_part, precision=highest) - jnp.einsum("mn,ncqd->mcqd", mech_imag, imag_part, precision=highest)
    new_imag = jnp.einsum("mn,ncqd->mcqd", mech_real, imag_part, precision=highest) + jnp.einsum("mn,ncqd->mcqd", mech_imag, real_part, precision=highest)
    return new_real, new_imag


def mech_bras(real_part, imag_part, mech_real, mech_imag):
    new_real = jnp.einsum("mcnd,qn->mcqd", real_part, mech_real, precision=highest) + jnp.einsum("mcnd,qn->mcqd", imag_part, mech_imag, precision=highest)
    new_imag = jnp.einsum("mcnd,qn->mcqd", imag_part, mech_real, precision=highest) - jnp.einsum("mcnd,qn->mcqd", real_part, mech_imag, precision=highest)
    return new_real, new_imag


def from_blocks(array):
    local_rows = MECH // N_ROW
    local_cols = MECH // N_COL
    shaped = array.reshape(N_ROW, N_COL, local_rows, CAV, local_cols, CAV)
    return jnp.transpose(shaped, (0, 2, 3, 1, 4, 5)).reshape(MECH, CAV, MECH, CAV)


def to_blocks(array):
    local_rows = MECH // N_ROW
    local_cols = MECH // N_COL
    shaped = array.reshape(N_ROW, local_rows, CAV, N_COL, local_cols, CAV)
    return jnp.transpose(shaped, (0, 3, 1, 2, 4, 5)).reshape(N_ROW, N_COL, local_rows * CAV * local_cols * CAV)


def reference(rho_real, rho_imag, cav_real, cav_imag, mech_real, mech_imag):
    real_part = from_blocks(rho_real)
    imag_part = from_blocks(rho_imag)
    for step in range(STEPS):
        real_part, imag_part = cavity_sides(real_part, imag_part, cav_real, cav_imag)
        real_part, imag_part = mech_kets(real_part, imag_part, mech_real, mech_imag)
        real_part, imag_part = mech_bras(real_part, imag_part, mech_real, mech_imag)
    return to_blocks(real_part), to_blocks(imag_part)
```

```python
import functools
import math

import jax
import jax.numpy as jnp
from jax import lax
from jax.experimental import pallas as pl
from jax.experimental.pallas import tpu as pltpu
from jax.sharding import PartitionSpec as P

highest = lax.Precision.HIGHEST


def cavity_sides(parts, cav_real, cav_imag):
    real_part, imag_part = parts
    left_real = jnp.einsum("cd,mdne->mcne", cav_real, real_part, precision=highest) - jnp.einsum(
        "cd,mdne->mcne", cav_imag, imag_part, precision=highest
    )
    left_imag = jnp.einsum("cd,mdne->mcne", cav_real, imag_part, precision=highest) + jnp.einsum(
        "cd,mdne->mcne", cav_imag, real_part, precision=highest
    )
    right_real = jnp.einsum("mcne,fe->mcnf", left_real, cav_real, precision=highest) + jnp.einsum(
        "mcne,fe->mcnf", left_imag, cav_imag, precision=highest
    )
    right_imag = jnp.einsum("mcne,fe->mcnf", left_imag, cav_real, precision=highest) - jnp.einsum(
        "mcne,fe->mcnf", left_real, cav_imag, precision=highest
    )
    return (right_real, right_imag)


def mech_mix(pieces, mech_real, mech_imag, adjoint):
    real_part, imag_part = pieces
    plain_rr = jnp.einsum("mn,nok->mok", mech_real, real_part, precision=highest)
    plain_ii = jnp.einsum("mn,nok->mok", mech_imag, imag_part, precision=highest)
    plain_ri = jnp.einsum("mn,nok->mok", mech_real, imag_part, precision=highest)
    plain_ir = jnp.einsum("mn,nok->mok", mech_imag, real_part, precision=highest)
    if adjoint:
        return (plain_rr + plain_ii, plain_ri - plain_ir)
    return (plain_rr - plain_ii, plain_ri + plain_ir)


def ket_side(parts, mech_real, mech_imag):
    real_part, imag_part = parts
    local_rows, cav_count, local_cols, width = real_part.shape
    groups = lax.axis_size("row")
    flat = cav_count * local_cols * width
    shaped = (
        real_part.reshape(local_rows, groups, flat // groups),
        imag_part.reshape(local_rows, groups, flat // groups),
    )
    mixed = mech_mix(
        (
            lax.all_to_all(shaped[0], "row", split_axis=1, concat_axis=0, tiled=True),
            lax.all_to_all(shaped[1], "row", split_axis=1, concat_axis=0, tiled=True),
        ),
        mech_real,
        mech_imag,
        False,
    )
    return (
        lax.all_to_all(mixed[0], "row", split_axis=0, concat_axis=1, tiled=True).reshape(
            local_rows, cav_count, local_cols, width
        ),
        lax.all_to_all(mixed[1], "row", split_axis=0, concat_axis=1, tiled=True).reshape(
            local_rows, cav_count, local_cols, width
        ),
    )


def bra_side(parts, mech_real, mech_imag):
    real_part, imag_part = parts
    local_rows, cav_count, local_cols, width = real_part.shape
    groups = lax.axis_size("col")
    flat = local_rows * cav_count * width
    moved_real = jnp.transpose(real_part, (2, 0, 1, 3)).reshape(local_cols, groups, flat // groups)
    moved_imag = jnp.transpose(imag_part, (2, 0, 1, 3)).reshape(local_cols, groups, flat // groups)
    mixed = mech_mix(
        (
            lax.all_to_all(moved_real, "col", split_axis=1, concat_axis=0, tiled=True),
            lax.all_to_all(moved_imag, "col", split_axis=1, concat_axis=0, tiled=True),
        ),
        mech_real,
        mech_imag,
        True,
    )
    back_real = jnp.transpose(
        lax.all_to_all(mixed[0], "col", split_axis=0, concat_axis=1, tiled=True).reshape(
            local_cols, local_rows, cav_count, width
        ),
        (1, 2, 0, 3),
    )
    back_imag = jnp.transpose(
        lax.all_to_all(mixed[1], "col", split_axis=0, concat_axis=1, tiled=True).reshape(
            local_cols, local_rows, cav_count, width
        ),
        (1, 2, 0, 3),
    )
    return (back_real, back_imag)


def general_local(rho_real, rho_imag, cav_real, cav_imag, mech_real, mech_imag):
    block_shape = rho_real.shape
    cav_count = cav_real.shape[0]
    local_rows = mech_real.shape[0] // lax.axis_size("row")
    local_cols = mech_real.shape[0] // lax.axis_size("col")
    shape_four = (local_rows, cav_count, local_cols, cav_count)
    state = (rho_real.reshape(shape_four), rho_imag.reshape(shape_four))
    state = cavity_sides(state, cav_real, cav_imag)
    state = bra_side(ket_side(state, mech_real, mech_imag), mech_real, mech_imag)
    return (state[0].reshape(block_shape), state[1].reshape(block_shape))


LANES = 128
SUB = 8


def set_pieces(groups, size):
    uppers, diagonals = pair_tables(groups)
    table = []
    for i, j in uppers:
        rows = [[(size * k, size * i + k, size * j)] for k in range(size)]
        table.append((rows, rows))
    for i, j in diagonals:
        first, second = [], []
        for k in range(size):
            low, high = (size * k, size * j + k, size * j), (size * i + k, size * i)
            first.append(([low] if k else []) + [(size * k + k,) + (high[0], high[1] + k)])
            upper = [(size * k + k + 1, high[0], high[1] + k + 1)] if k + 1 < size else []
            second.append([low] + upper)
        table.append((first, second))
    return table


def split_high(value):
    high = value.astype(jnp.bfloat16)
    return high, (value - high.astype(jnp.float32)).astype(jnp.bfloat16)


def split_weights(value):
    high = lax.reduce_precision(value, exponent_bits=8, mantissa_bits=7)
    return high.astype(jnp.bfloat16), (value - high).astype(jnp.bfloat16)


def dot3(left, right):
    total = jnp.dot(left[0], right[1], preferred_element_type=jnp.float32)
    total += jnp.dot(left[1], right[0], preferred_element_type=jnp.float32)
    return total + jnp.dot(left[0], right[0], preferred_element_type=jnp.float32)


def lane_index():
    return lax.broadcasted_iota(jnp.int32, (SUB, LANES), 1)


def turn(value, shift):
    return pltpu.roll(value, shift % LANES, 1) if shift % LANES else value


def enter_kernel(dims, *refs):
    cav, cols, period, pad, chunks = dims
    x_refs, (lh, ll, rh, rl) = refs[:2], refs[2:6]
    outs = refs[6 : 6 + chunks]
    work, plain, turned = refs[6 + chunks :]
    lane = lane_index()
    stride = x_refs[0].shape[0] // SUB
    step_rows = period * cols * cav // LANES
    count = cols * SUB

    @pl.when(pl.program_id(0) == 0)
    def _():
        work[...] = jnp.zeros_like(work)

    def unroll(outer, carry):
        for part in range(2):
            for inner in range(period):
                for col in range(cols):
                    place = (inner * cols + col) * cav
                    row, shift = outer * step_rows + place // LANES, place % LANES
                    value = x_refs[part][pl.ds(row, SUB, stride=stride), :]
                    if shift + cav > LANES:
                        after = x_refs[part][pl.ds(row + 1, SUB, stride=stride), :]
                        value = jnp.where(lane >= shift, value, after)
                    target = col * SUB * pad + outer * period + inner
                    work[part, pl.ds(target, SUB, stride=pad), :] = turn(value, -shift)
        return carry

    lax.fori_loop(0, cav // period, unroll, 0)

    left = (lh[...], ll[...])
    right = (rh[...], rl[...])

    def mix(pair, carry):
        halves = []
        for extra in range(2):
            start = pl.multiple_of((2 * pair + extra) * pad, SUB)
            halves.append(jnp.concatenate([work[0, pl.ds(start, pad), :], work[1, pl.ds(start, pad), :]], axis=0))
        ket = dot3(left, split_high(jnp.concatenate(halves, axis=1)))
        stacked = jnp.concatenate(
            [
                jnp.concatenate([ket[:pad, lo : lo + LANES], ket[LANES : LANES + pad, lo : lo + LANES]], axis=1)
                for lo in (0, LANES)
            ],
            axis=0,
        )
        both = dot3(split_high(stacked), right)
        for extra in range(2):
            for part in range(2):
                block = both[extra * pad : (extra + 1) * pad, part * LANES : (part + 1) * LANES]
                plain[part, pl.ds(2 * pair + extra, pad, stride=count), :] = block
                square = jnp.concatenate([block, jnp.zeros((LANES - pad, LANES), jnp.float32)], axis=0)
                turned[part, pl.ds(2 * pair + extra, pad, stride=count), :] = jnp.transpose(square)[:pad]
        return carry

    lax.fori_loop(0, count // 2, mix, 0)

    size = cav // 4
    table = set_pieces(4, size)
    end = size * size

    def gather(col, carry):
        for chunk in range(chunks):
            base = chunk * LANES
            for index, pair in enumerate(table):
                for side in range(2):
                    source = (plain, turned)[side]
                    pieces = [piece for row in pair[side] for piece in row]
                    for part in range(2):
                        total = None
                        for at, (first, row, lane_from) in enumerate(pieces):
                            last = pieces[at + 1][0] if at + 1 < len(pieces) else end
                            if last <= base or first >= base + LANES:
                                continue
                            start = pl.multiple_of(row * count + col * SUB, SUB)
                            value = turn(source[part, pl.ds(start, SUB), :], first - base - lane_from)
                            total = value if total is None else jnp.where(lane >= first - base, value, total)
                        if end < base + LANES:
                            total = jnp.where(lane < end - base, total, 0.0)
                        outs[chunk][index, side, part, col] = total
        return carry

    lax.fori_loop(0, cols, gather, 0)


def leave_kernel(dims, *refs):
    cav, cols, period, pad, chunks = dims
    ins, outs = refs[:chunks], refs[chunks : chunks + 2]
    plain, turned = refs[chunks + 2 :]
    lane = lane_index()
    count = cols * SUB
    size = cav // 4
    groups = 4
    table = set_pieces(groups, size)
    end = size * size

    def scatter(col, carry):
        for side in range(2):
            target = (plain, turned)[side]
            found = [[] for _ in range(cav)]
            for index, pair in enumerate(table):
                pieces = [piece for row in pair[side] for piece in row]
                for at, (first, row, lane_from) in enumerate(pieces):
                    last = pieces[at + 1][0] if at + 1 < len(pieces) else end
                    while first < last:
                        stop = min(last, (first // LANES + 1) * LANES)
                        found[row].append((lane_from, stop - first, index, first))
                        lane_from, first = lane_from + stop - first, stop
            for row in range(cav):
                for part in range(2):
                    total, reach = None, 0
                    for lane_to, length, index, first in sorted(found[row]):
                        if total is None:
                            total = jnp.zeros((SUB, LANES), jnp.float32)
                        elif lane_to > reach:
                            total = jnp.where(lane >= reach, 0.0, total)
                        value = turn(ins[first // LANES][index, side, part, col], lane_to - first % LANES)
                        total = jnp.where(lane >= lane_to, value, total)
                        reach = lane_to + length
                    if total is None:
                        total = jnp.zeros((SUB, LANES), jnp.float32)
                    else:
                        total = jnp.where(lane < reach, total, 0.0)
                    start = pl.multiple_of(row * count + col * SUB, SUB)
                    target[part, pl.ds(start, SUB), :] = total
        return carry

    lax.fori_loop(0, cols, scatter, 0)

    def merge(index, carry):
        for part in range(2):
            block = turned[part, pl.ds(index, pad, stride=count), :]
            square = jnp.concatenate([block, jnp.zeros((LANES - pad, LANES), jnp.float32)], axis=0)
            rows = pl.ds(index, pad, stride=count)
            plain[part, rows, :] = plain[part, rows, :] + jnp.transpose(square)[:pad]
        return carry

    lax.fori_loop(0, count, merge, 0)

    stride = outs[0].shape[0] // SUB
    step_rows = period * cols * cav // LANES

    def store(outer, carry):
        for part in range(2):
            for inner in range(step_rows):
                begin = inner * LANES
                total = None
                for piece in range(begin // cav, (begin + LANES - 1) // cav + 1):
                    row = (outer * period + piece // cols) * count + (piece % cols) * SUB
                    value = turn(plain[part, pl.ds(pl.multiple_of(row, SUB), SUB), :], piece * cav - begin)
                    total = value if total is None else jnp.where(lane >= piece * cav - begin, value, total)
                outs[part][pl.ds(outer * step_rows + inner, SUB, stride=stride), :] = total
        return carry

    lax.fori_loop(0, cav // period, store, 0)


def kernel_dims(cav, cols):
    period = LANES // math.gcd(cols * cav, LANES)
    pad = -(-cav // SUB) * SUB
    chunks = -(-(cav // 4) ** 2 // LANES)
    return cav, cols, period, pad, chunks


def kernels_fit(rows, cols, cav):
    period = LANES // math.gcd(cols * cav, LANES)
    return rows % SUB == 0 and cols % 2 == 0 and cav % 4 == 0 and cav % period == 0 and 4 * SUB <= cav <= LANES


def enter(x_real, x_imag, cav_real, cav_imag, rows, cols):
    cav = cav_real.shape[0]
    dims = kernel_dims(cav, cols)
    _, _, _, pad, chunks = dims
    lines = cav * cols * cav // LANES * SUB
    steps = rows // SUB

    def put(matrix, height, width):
        return jnp.pad(matrix, ((0, height - cav), (0, width - cav)))

    ket = jnp.block(
        [
            [put(cav_real, LANES, pad), put(-cav_imag, LANES, pad)],
            [put(cav_imag, LANES, pad), put(cav_real, LANES, pad)],
        ]
    )
    bra = jnp.block(
        [
            [put(cav_real.T, LANES, LANES), put(-cav_imag.T, LANES, LANES)],
            [put(cav_imag.T, LANES, LANES), put(cav_real.T, LANES, LANES)],
        ]
    )
    weights = split_weights(ket) + split_weights(bra)
    n_sets = 8
    shape = (n_sets, 2, 2, cols, rows, LANES)
    return pl.pallas_call(
        functools.partial(enter_kernel, dims),
        grid=(steps,),
        in_specs=[pl.BlockSpec((lines, LANES), lambda g: (g, 0))] * 2
        + [pl.BlockSpec(w.shape, lambda g: (0, 0)) for w in weights],
        out_specs=[pl.BlockSpec((n_sets, 2, 2, cols, SUB, LANES), lambda g: (0, 0, 0, 0, g, 0))] * chunks,
        out_shape=[jax.ShapeDtypeStruct(shape, jnp.float32)] * chunks,
        scratch_shapes=[
            pltpu.VMEM((2, cols * SUB * pad, LANES), jnp.float32),
            pltpu.VMEM((2, cols * SUB * pad, LANES), jnp.float32),
            pltpu.VMEM((2, cols * SUB * pad, LANES), jnp.float32),
        ],
        compiler_params=pltpu.CompilerParams(vmem_limit_bytes=60 * 1024 * 1024),
        name="enter",
    )(x_real, x_imag, *weights)


def leave(sets, cav, rows, cols):
    dims = kernel_dims(cav, cols)
    _, _, _, pad, chunks = dims
    lines = cav * cols * cav // LANES * SUB
    steps = rows // SUB
    n_sets = 8
    return pl.pallas_call(
        functools.partial(leave_kernel, dims),
        grid=(steps,),
        in_specs=[pl.BlockSpec((n_sets, 2, 2, cols, SUB, LANES), lambda g: (0, 0, 0, 0, g, 0))] * chunks,
        out_specs=[pl.BlockSpec((lines, LANES), lambda g: (g, 0))] * 2,
        out_shape=[jax.ShapeDtypeStruct((lines * steps, LANES), jnp.float32)] * 2,
        scratch_shapes=[
            pltpu.VMEM((2, cols * SUB * pad, LANES), jnp.float32),
            pltpu.VMEM((2, cols * SUB * pad, LANES), jnp.float32),
        ],
        compiler_params=pltpu.CompilerParams(vmem_limit_bytes=60 * 1024 * 1024),
        name="leave",
    )(*sets)


def pair_tables(groups):
    uppers = [(i, j) for i in range(groups) for j in range(i + 1, groups)]
    diagonals = [(2 * i, 2 * i + 1) for i in range(groups // 2)]
    return uppers, diagonals


def ket_kernel(base, flags, own_ref, wh_ref, wl_ref, row_ref, ends_ref, mids_ref, corner_ref, sent_ref, half_ref):
    halves, cols, rows = base
    width = halves * cols
    own = own_ref[0, :] > 0

    @pl.when(flags[1] == 0)
    def _():
        far = flags[0]

        def own_row(block):
            spot = lax.select(far == 1, 3 - block, block)

            def by_bra(side, part, n):
                return row_ref[spot * halves + n // cols, side, part, n % cols]

            def by_ket(side, part, m):
                pieces = [
                    row_ref.at[spot * halves + h, side, part].reshape(cols * rows, LANES)[pl.ds(m, cols, stride=rows), :]
                    for h in range(halves)
                ]
                return jnp.concatenate(pieces, axis=0)

            return by_bra, by_ket

        def got(ref, lead):
            view = ref if lead is None else ref.at[lead]

            def by_bra(side, part, n):
                return view[n // cols, side, part, n % cols]

            def by_ket(side, part, m):
                pieces = [
                    view.at[h, side, part].reshape(cols * rows, LANES)[pl.ds(m, cols, stride=rows), :]
                    for h in range(halves)
                ]
                return jnp.concatenate(pieces, axis=0)

            return by_bra, by_ket

        known = {
            (1, 0): own_row(0),
            (1, 1): own_row(1),
            (1, 2): own_row(2),
            (1, 3): own_row(3),
            (0, 0): got(ends_ref, 0),
            (0, 2): got(ends_ref, 1),
            (0, 3): got(ends_ref, 2),
            (2, 3): got(mids_ref, 0),
            (2, 2): got(mids_ref, 1),
            (3, 3): got(corner_ref, None),
        }
        weights = (wh_ref[...], wl_ref[...])

        for block in range(4):

            def step(n, carry, block=block):
                columns = []
                for side in range(2):
                    pieces = []
                    for part in range(2):
                        for p in range(4):
                            if (p, block) in known:
                                pieces.append(known[p, block][0](side, part, n))
                            else:
                                read = known[block, p][1]
                                value = jnp.where(own, read(side, part, n), read(1 - side, part, n))
                                pieces.append(-value if part else value)
                    columns.append(jnp.concatenate(pieces, axis=0))
                result = dot3(weights, split_high(jnp.concatenate(columns, axis=1)))
                for side in range(2):
                    lanes = slice(side * LANES, (side + 1) * LANES)
                    for part in range(2):
                        top = part * 2 * rows
                        if block:
                            sent_ref[side, part, (block - 1) * width + n] = result[top : top + rows, lanes]
                        half_ref[side, part, block * width + n] = result[top + rows : top + 2 * rows, lanes]
                return carry

            lax.fori_loop(0, width, step, 0)


def bra_kernel(base, flags, own_ref, eh_ref, el_ref, bh_ref, bl_ref, row_ref, part_ref, half_ref, out_ref, work):
    halves, cols, rows = base
    width = halves * cols
    mech = 4 * width
    own = own_ref[0, :] > 0
    far = flags[0]

    def spot_of(block):
        return lax.select(far == 1, 3 - block, block)

    @pl.when(flags[1] == 1)
    def _():
        def by_ket(block, side, part, m):
            pieces = [
                row_ref.at[spot_of(block) * halves + h, side, part].reshape(cols * rows, LANES)[
                    pl.ds(m, cols, stride=rows), :
                ]
                for h in range(halves)
            ]
            return jnp.concatenate(pieces, axis=0)

        weights = (eh_ref[...], el_ref[...])

        for block in range(4):

            def step(n, carry, block=block):
                columns = []
                for side in range(2):
                    pieces = []
                    for part in range(2):
                        pieces.append(row_ref[spot_of(block) * halves + n // cols, side, part, n % cols])
                        for p in range(1, 4):
                            if block:
                                pieces.append(jnp.zeros((rows, LANES), jnp.float32))
                            else:
                                value = jnp.where(own, by_ket(p, side, part, n), by_ket(p, 1 - side, part, n))
                                pieces.append(-value if part else value)
                    columns.append(jnp.concatenate(pieces, axis=0))
                result = dot3(weights, split_high(jnp.concatenate(columns, axis=1)))
                for side in range(2):
                    for part in range(2):
                        value = result[part * rows : (part + 1) * rows, side * LANES : (side + 1) * LANES]
                        if block:
                            value = value + part_ref[side, part, (block - 1) * width + n]
                        work[side, part, pl.ds(pl.multiple_of((block * width + n) * rows, SUB), rows), :] = value
                return carry

            lax.fori_loop(0, width, step, 0)

    @pl.when(flags[1] == 0)
    def _():
        def step(n, carry):
            for side in range(2):
                for part in range(2):
                    work[side, part, pl.ds(pl.multiple_of(n * rows, SUB), rows), :] = half_ref[side, part, n]
            return carry

        lax.fori_loop(0, mech, step, 0)

    weights = (bh_ref[...], bl_ref[...])

    def finish(m, carry):
        columns = [
            jnp.concatenate([work[side, part, pl.ds(m, mech, stride=rows), :] for part in range(2)], axis=0)
            for side in range(2)
        ]
        result = dot3(weights, split_high(jnp.concatenate(columns, axis=1)))
        for side in range(2):
            for part in range(2):
                value = result[part * mech : (part + 1) * mech, side * LANES : (side + 1) * LANES]
                work[side, part, pl.ds(m, mech, stride=rows), :] = value
        return carry

    lax.fori_loop(0, rows, finish, 0)

    def put(q, carry):
        spot = lax.select(far == 1, 3 - q // width, q // width)
        for side in range(2):
            for part in range(2):
                value = work[side, part, pl.ds(pl.multiple_of(q * rows, SUB), rows), :]
                out_ref[spot * halves + q % width // cols, side, part, q % cols] = value
        return carry

    lax.fori_loop(0, mech, put, 0)


def whole_block(shape):
    return pl.BlockSpec(shape, lambda g, flags: (0,) * len(shape))


LIMIT = 48 * 1024 * 1024


def send_blocks(got, flags):
    inner = [(0, 1), (3, 2)]
    cross = [(1, 2), (2, 1)]
    halves = got.shape[0] // 4
    far = flags[0] == 1

    def block_of(index):
        return lax.dynamic_slice_in_dim(got, jnp.where(far, 3 - index, index) * halves, halves, 0)

    ends = lax.ppermute(jnp.stack([block_of(0), block_of(2), block_of(3)]), "row", inner)
    mids = lax.ppermute(jnp.stack([block_of(0), block_of(1)]), "row", cross)
    corner = lax.ppermute(ends[0], "row", cross)
    return ends, mids, corner


def mix_kets(got, ends, mids, corner, own, flags, weights):
    members, _, _, cols, rows, _ = got.shape
    halves = members // 4
    width = halves * cols
    args = (own, weights[0], weights[1], got, ends, mids, corner)
    shapes = ((2, 2, 3 * width, rows, LANES), (2, 2, 4 * width, rows, LANES))
    sent, half = pl.pallas_call(
        functools.partial(ket_kernel, (halves, cols, rows)),
        grid_spec=pltpu.PrefetchScalarGridSpec(
            num_scalar_prefetch=1,
            grid=(1,),
            in_specs=[whole_block(a.shape) for a in args],
            out_specs=[whole_block(shape) for shape in shapes],
        ),
        out_shape=[jax.ShapeDtypeStruct(shape, jnp.float32) for shape in shapes],
        compiler_params=pltpu.CompilerParams(vmem_limit_bytes=LIMIT),
        cost_estimate=pl.CostEstimate(flops=12_000_000_000, bytes_accessed=40_000_000, transcendentals=0),
        name="ket",
    )(flags, *args)
    return lax.ppermute(sent, "row", [(1, 0), (2, 3)]), half


def mix_bras(got, partial, half, own, flags, end_line, bra):
    members, _, _, cols, rows, _ = got.shape
    halves = members // 4
    args = (own, end_line[0], end_line[1], bra[0], bra[1], got, partial, half)
    return pl.pallas_call(
        functools.partial(bra_kernel, (halves, cols, rows)),
        grid_spec=pltpu.PrefetchScalarGridSpec(
            num_scalar_prefetch=1,
            grid=(1,),
            in_specs=[whole_block(a.shape) for a in args],
            out_specs=whole_block(got.shape),
            scratch_shapes=[pltpu.VMEM((2, 2, members * cols * rows, LANES), jnp.float32)],
        ),
        out_shape=jax.ShapeDtypeStruct(got.shape, jnp.float32),
        compiler_params=pltpu.CompilerParams(vmem_limit_bytes=LIMIT),
        cost_estimate=pl.CostEstimate(flops=12_000_000_000, bytes_accessed=40_000_000, transcendentals=0),
        name="bra",
    )(flags, *args)


def swap_plane(array):
    return lax.all_to_all(array, "col", split_axis=0, concat_axis=0, tiled=True)


def realified(real_part, imag_part, sign):
    top = jnp.concatenate([real_part, -sign * imag_part], axis=1)
    bottom = jnp.concatenate([sign * imag_part, real_part], axis=1)
    return split_weights(jnp.concatenate([top, bottom], axis=0))


def fast_local(rho_real, rho_imag, cav_real, cav_imag, mech_real, mech_imag):
    block_shape = rho_real.shape
    cav = cav_real.shape[0]
    mech = mech_real.shape[0]
    n_row, n_col = lax.axis_size("row"), lax.axis_size("col")
    rows, cols = mech // n_row, mech // n_col
    size = cav // n_row
    sets = enter(
        rho_real.reshape(-1, LANES), rho_imag.reshape(-1, LANES), cav_real, cav_imag, rows, cols
    )
    chunks = len(sets)

    place = lax.axis_index("row")
    member = lax.axis_index("col")
    far_half = place >= n_row // 2
    is_end = (place == 0) | (place == n_row - 1)
    flags = jnp.stack([far_half, is_end]).astype(jnp.int32)
    lanes = jnp.arange(chunks * LANES)
    uppers, _ = pair_tables(n_row)
    own_lanes = ((member >= len(uppers)) & ((lanes // size) == (lanes % size))).astype(jnp.int32)

    def order(matrix):
        shaped = matrix.reshape(n_row, rows, n_row, rows)
        return jnp.where(far_half, shaped[::-1, :, ::-1], shaped).reshape(mech, mech)

    mixer_real, mixer_imag = order(mech_real), order(mech_imag)
    outside = (jnp.arange(mech) >= rows)[None, :]
    away_real = jnp.where(outside, mixer_real[:rows], 0.0)
    away_imag = jnp.where(outside, mixer_imag[:rows], 0.0)
    whole = realified(
        jnp.concatenate([away_real, mixer_real[rows : 2 * rows]]),
        jnp.concatenate([away_imag, mixer_imag[rows : 2 * rows]]),
        1.0,
    )
    end_line = realified(mixer_real[:rows], mixer_imag[:rows], 1.0)
    bra = realified(mixer_real, mixer_imag, -1.0)
    own = [own_lanes[chunk * LANES : (chunk + 1) * LANES][None] for chunk in range(chunks)]

    state = {("set", chunk): sets[chunk] for chunk in range(chunks)}
    for tick in range(chunks + 3):
        made = {}
        if tick < chunks:
            made["row", tick] = swap_plane(state.pop(("set", tick)))
        if 0 <= tick - 1 < chunks:
            made["sent", tick - 1] = send_blocks(state["row", tick - 1], flags)
        if 0 <= tick - 2 < chunks:
            at = tick - 2
            made["half", at] = mix_kets(state["row", at], *state.pop(("sent", at)), own[at], flags, whole)
        if 0 <= tick - 3 < chunks:
            at = tick - 3
            row = state.pop(("row", at))
            out = mix_bras(row, *state.pop(("half", at)), own[at], flags, end_line, bra)
            made["done", at] = swap_plane(out)
        state.update(made)
        names = sorted(state)
        state = dict(zip(names, lax.optimization_barrier([state[name] for name in names])))
    results = [state["done", chunk] for chunk in range(chunks)]
    final = leave(results, cav, rows, cols)
    return final[0].reshape(block_shape), final[1].reshape(block_shape)


def fits(mesh, mech, cav):
    n_row, n_col = mesh.shape["row"], mesh.shape["col"]
    if n_row != 4 or n_col != 2 * n_row or mech % n_col:
        return False
    return kernels_fit(mech // n_row, mech // n_col, cav)


def solution(mesh):
    def whole(rho_real, rho_imag, cav_real, cav_imag, mech_real, mech_imag):
        local = fast_local if fits(mesh, mech_real.shape[0], cav_real.shape[0]) else general_local
        return jax.shard_map(
            local,
            mesh=mesh,
            in_specs=(P("row", "col", None), P("row", "col", None), P(), P(), P(), P()),
            out_specs=(P("row", "col", None), P("row", "col", None)),
            check_vma=False,
        )(rho_real, rho_imag, cav_real, cav_imag, mech_real, mech_imag)

    return whole
```

```python
import functools
import math

import jax
import jax.numpy as jnp
from jax import lax
from jax.experimental import pallas as pl
from jax.experimental.pallas import tpu as pltpu
from jax.sharding import PartitionSpec as P

highest = lax.Precision.HIGHEST


def cavity_sides(parts, cav_real, cav_imag):
    real_part, imag_part = parts
    left_real = jnp.einsum("cd,mdne->mcne", cav_real, real_part, precision=highest) - jnp.einsum(
        "cd,mdne->mcne", cav_imag, imag_part, precision=highest
    )
    left_imag = jnp.einsum("cd,mdne->mcne", cav_real, imag_part, precision=highest) + jnp.einsum(
        "cd,mdne->mcne", cav_imag, real_part, precision=highest
    )
    right_real = jnp.einsum("mcne,fe->mcnf", left_real, cav_real, precision=highest) + jnp.einsum(
        "mcne,fe->mcnf", left_imag, cav_imag, precision=highest
    )
    right_imag = jnp.einsum("mcne,fe->mcnf", left_imag, cav_real, precision=highest) - jnp.einsum(
        "mcne,fe->mcnf", left_real, cav_imag, precision=highest
    )
    return (right_real, right_imag)


def mech_mix(pieces, mech_real, mech_imag, adjoint):
    real_part, imag_part = pieces
    plain_rr = jnp.einsum("mn,nok->mok", mech_real, real_part, precision=highest)
    plain_ii = jnp.einsum("mn,nok->mok", mech_imag, imag_part, precision=highest)
    plain_ri = jnp.einsum("mn,nok->mok", mech_real, imag_part, precision=highest)
    plain_ir = jnp.einsum("mn,nok->mok", mech_imag, real_part, precision=highest)
    if adjoint:
        return (plain_rr + plain_ii, plain_ri - plain_ir)
    return (plain_rr - plain_ii, plain_ri + plain_ir)


def ket_side(parts, mech_real, mech_imag):
    real_part, imag_part = parts
    local_rows, cav_count, local_cols, width = real_part.shape
    groups = lax.axis_size("row")
    flat = cav_count * local_cols * width
    shaped = (
        real_part.reshape(local_rows, groups, flat // groups),
        imag_part.reshape(local_rows, groups, flat // groups),
    )
    mixed = mech_mix(
        (
            lax.all_to_all(shaped[0], "row", split_axis=1, concat_axis=0, tiled=True),
            lax.all_to_all(shaped[1], "row", split_axis=1, concat_axis=0, tiled=True),
        ),
        mech_real,
        mech_imag,
        False,
    )
    return (
        lax.all_to_all(mixed[0], "row", split_axis=0, concat_axis=1, tiled=True).reshape(
            local_rows, cav_count, local_cols, width
        ),
        lax.all_to_all(mixed[1], "row", split_axis=0, concat_axis=1, tiled=True).reshape(
            local_rows, cav_count, local_cols, width
        ),
    )


def bra_side(parts, mech_real, mech_imag):
    real_part, imag_part = parts
    local_rows, cav_count, local_cols, width = real_part.shape
    groups = lax.axis_size("col")
    flat = local_rows * cav_count * width
    moved_real = jnp.transpose(real_part, (2, 0, 1, 3)).reshape(local_cols, groups, flat // groups)
    moved_imag = jnp.transpose(imag_part, (2, 0, 1, 3)).reshape(local_cols, groups, flat // groups)
    mixed = mech_mix(
        (
            lax.all_to_all(moved_real, "col", split_axis=1, concat_axis=0, tiled=True),
            lax.all_to_all(moved_imag, "col", split_axis=1, concat_axis=0, tiled=True),
        ),
        mech_real,
        mech_imag,
        True,
    )
    back_real = jnp.transpose(
        lax.all_to_all(mixed[0], "col", split_axis=0, concat_axis=1, tiled=True).reshape(
            local_cols, local_rows, cav_count, width
        ),
        (1, 2, 0, 3),
    )
    back_imag = jnp.transpose(
        lax.all_to_all(mixed[1], "col", split_axis=0, concat_axis=1, tiled=True).reshape(
            local_cols, local_rows, cav_count, width
        ),
        (1, 2, 0, 3),
    )
    return (back_real, back_imag)


def general_local(rho_real, rho_imag, cav_real, cav_imag, mech_real, mech_imag):
    block_shape = rho_real.shape
    cav_count = cav_real.shape[0]
    local_rows = mech_real.shape[0] // lax.axis_size("row")
    local_cols = mech_real.shape[0] // lax.axis_size("col")
    shape_four = (local_rows, cav_count, local_cols, cav_count)
    state = (rho_real.reshape(shape_four), rho_imag.reshape(shape_four))
    state = cavity_sides(state, cav_real, cav_imag)
    state = bra_side(ket_side(state, mech_real, mech_imag), mech_real, mech_imag)
    return (state[0].reshape(block_shape), state[1].reshape(block_shape))


LANES = 128
SUB = 8


def set_pieces(groups, size):
    uppers, diagonals = pair_tables(groups)
    table = []
    for i, j in uppers:
        rows = [[(size * k, size * i + k, size * j)] for k in range(size)]
        table.append((rows, rows))
    for i, j in diagonals:
        first, second = [], []
        for k in range(size):
            low, high = (size * k, size * j + k, size * j), (size * i + k, size * i)
            first.append(([low] if k else []) + [(size * k + k,) + (high[0], high[1] + k)])
            upper = [(size * k + k + 1, high[0], high[1] + k + 1)] if k + 1 < size else []
            second.append([low] + upper)
        table.append((first, second))
    return table


def split_high(value):
    high = value.astype(jnp.bfloat16)
    return high, (value - high.astype(jnp.float32)).astype(jnp.bfloat16)


def split_weights(value):
    high = lax.reduce_precision(value, exponent_bits=8, mantissa_bits=7)
    return high.astype(jnp.bfloat16), (value - high).astype(jnp.bfloat16)


def dot3(left, right):
    total = jnp.dot(left[0], right[1], preferred_element_type=jnp.float32)
    total += jnp.dot(left[1], right[0], preferred_element_type=jnp.float32)
    return total + jnp.dot(left[0], right[0], preferred_element_type=jnp.float32)


def lane_index():
    return lax.broadcasted_iota(jnp.int32, (SUB, LANES), 1)


def turn(value, shift):
    return pltpu.roll(value, shift % LANES, 1) if shift % LANES else value


def enter_kernel(dims, *refs):
    cav, cols, period, pad, chunks = dims
    x_refs, (lh, ll, rh, rl) = refs[:2], refs[2:6]
    outs = refs[6 : 6 + chunks]
    work, plain, turned = refs[6 + chunks :]
    lane = lane_index()
    stride = x_refs[0].shape[0] // SUB
    step_rows = period * cols * cav // LANES
    count = cols * SUB

    @pl.when(pl.program_id(0) == 0)
    def _():
        work[...] = jnp.zeros_like(work)

    def unroll(outer, carry):
        for part in range(2):
            for inner in range(period):
                for col in range(cols):
                    place = (inner * cols + col) * cav
                    row, shift = outer * step_rows + place // LANES, place % LANES
                    value = x_refs[part][pl.ds(row, SUB, stride=stride), :]
                    if shift + cav > LANES:
                        after = x_refs[part][pl.ds(row + 1, SUB, stride=stride), :]
                        value = jnp.where(lane >= shift, value, after)
                    target = col * SUB * pad + outer * period + inner
                    work[part, pl.ds(target, SUB, stride=pad), :] = turn(value, -shift)
        return carry

    lax.fori_loop(0, cav // period, unroll, 0)

    left = (lh[...], ll[...])
    right = (rh[...], rl[...])

    def mix(pair, carry):
        halves = []
        for extra in range(2):
            start = pl.multiple_of((2 * pair + extra) * pad, SUB)
            halves.append(jnp.concatenate([work[0, pl.ds(start, pad), :], work[1, pl.ds(start, pad), :]], axis=0))
        ket = dot3(left, split_high(jnp.concatenate(halves, axis=1)))
        stacked = jnp.concatenate(
            [
                jnp.concatenate([ket[:pad, lo : lo + LANES], ket[LANES : LANES + pad, lo : lo + LANES]], axis=1)
                for lo in (0, LANES)
            ],
            axis=0,
        )
        both = dot3(split_high(stacked), right)
        for extra in range(2):
            for part in range(2):
                block = both[extra * pad : (extra + 1) * pad, part * LANES : (part + 1) * LANES]
                plain[part, pl.ds(2 * pair + extra, pad, stride=count), :] = block
                square = jnp.concatenate([block, jnp.zeros((LANES - pad, LANES), jnp.float32)], axis=0)
                turned[part, pl.ds(2 * pair + extra, pad, stride=count), :] = jnp.transpose(square)[:pad]
        return carry

    lax.fori_loop(0, count // 2, mix, 0)

    size = cav // 4
    table = set_pieces(4, size)
    end = size * size

    def gather(col, carry):
        for chunk in range(chunks):
            base = chunk * LANES
            for index, pair in enumerate(table):
                for side in range(2):
                    source = (plain, turned)[side]
                    pieces = [piece for row in pair[side] for piece in row]
                    for part in range(2):
                        total = None
                        for at, (first, row, lane_from) in enumerate(pieces):
                            last = pieces[at + 1][0] if at + 1 < len(pieces) else end
                            if last <= base or first >= base + LANES:
                                continue
                            start = pl.multiple_of(row * count + col * SUB, SUB)
                            value = turn(source[part, pl.ds(start, SUB), :], first - base - lane_from)
                            total = value if total is None else jnp.where(lane >= first - base, value, total)
                        if end < base + LANES:
                            total = jnp.where(lane < end - base, total, 0.0)
                        outs[chunk][index, side, part, col] = total
        return carry

    lax.fori_loop(0, cols, gather, 0)


def leave_kernel(dims, *refs):
    cav, cols, period, pad, chunks = dims
    ins, outs = refs[:chunks], refs[chunks : chunks + 2]
    plain, turned = refs[chunks + 2 :]
    lane = lane_index()
    count = cols * SUB
    size = cav // 4
    groups = 4
    table = set_pieces(groups, size)
    end = size * size

    def scatter(col, carry):
        for side in range(2):
            target = (plain, turned)[side]
            found = [[] for _ in range(cav)]
            for index, pair in enumerate(table):
                pieces = [piece for row in pair[side] for piece in row]
                for at, (first, row, lane_from) in enumerate(pieces):
                    last = pieces[at + 1][0] if at + 1 < len(pieces) else end
                    while first < last:
                        stop = min(last, (first // LANES + 1) * LANES)
                        found[row].append((lane_from, stop - first, index, first))
                        lane_from, first = lane_from + stop - first, stop
            for row in range(cav):
                for part in range(2):
                    total, reach = None, 0
                    for lane_to, length, index, first in sorted(found[row]):
                        if total is None:
                            total = jnp.zeros((SUB, LANES), jnp.float32)
                        elif lane_to > reach:
                            total = jnp.where(lane >= reach, 0.0, total)
                        value = turn(ins[first // LANES][index, side, part, col], lane_to - first % LANES)
                        total = jnp.where(lane >= lane_to, value, total)
                        reach = lane_to + length
                    if total is None:
                        total = jnp.zeros((SUB, LANES), jnp.float32)
                    else:
                        total = jnp.where(lane < reach, total, 0.0)
                    start = pl.multiple_of(row * count + col * SUB, SUB)
                    target[part, pl.ds(start, SUB), :] = total
        return carry

    lax.fori_loop(0, cols, scatter, 0)

    def merge(index, carry):
        for part in range(2):
            block = turned[part, pl.ds(index, pad, stride=count), :]
            square = jnp.concatenate([block, jnp.zeros((LANES - pad, LANES), jnp.float32)], axis=0)
            rows = pl.ds(index, pad, stride=count)
            plain[part, rows, :] = plain[part, rows, :] + jnp.transpose(square)[:pad]
        return carry

    lax.fori_loop(0, count, merge, 0)

    stride = outs[0].shape[0] // SUB
    step_rows = period * cols * cav // LANES

    def store(outer, carry):
        for part in range(2):
            for inner in range(step_rows):
                begin = inner * LANES
                total = None
                for piece in range(begin // cav, (begin + LANES - 1) // cav + 1):
                    row = (outer * period + piece // cols) * count + (piece % cols) * SUB
                    value = turn(plain[part, pl.ds(pl.multiple_of(row, SUB), SUB), :], piece * cav - begin)
                    total = value if total is None else jnp.where(lane >= piece * cav - begin, value, total)
                outs[part][pl.ds(outer * step_rows + inner, SUB, stride=stride), :] = total
        return carry

    lax.fori_loop(0, cav // period, store, 0)


def kernel_dims(cav, cols):
    period = LANES // math.gcd(cols * cav, LANES)
    pad = -(-cav // SUB) * SUB
    chunks = -(-(cav // 4) ** 2 // LANES)
    return cav, cols, period, pad, chunks


def kernels_fit(rows, cols, cav):
    period = LANES // math.gcd(cols * cav, LANES)
    return rows % SUB == 0 and cols % 2 == 0 and cav % 4 == 0 and cav % period == 0 and 4 * SUB <= cav <= LANES


def enter(x_real, x_imag, cav_real, cav_imag, rows, cols):
    cav = cav_real.shape[0]
    dims = kernel_dims(cav, cols)
    _, _, _, pad, chunks = dims
    lines = cav * cols * cav // LANES * SUB
    steps = rows // SUB

    def put(matrix, height, width):
        return jnp.pad(matrix, ((0, height - cav), (0, width - cav)))

    ket = jnp.block(
        [
            [put(cav_real, LANES, pad), put(-cav_imag, LANES, pad)],
            [put(cav_imag, LANES, pad), put(cav_real, LANES, pad)],
        ]
    )
    bra = jnp.block(
        [
            [put(cav_real.T, LANES, LANES), put(-cav_imag.T, LANES, LANES)],
            [put(cav_imag.T, LANES, LANES), put(cav_real.T, LANES, LANES)],
        ]
    )
    weights = split_weights(ket) + split_weights(bra)
    n_sets = 8
    shape = (n_sets, 2, 2, cols, rows, LANES)
    return pl.pallas_call(
        functools.partial(enter_kernel, dims),
        grid=(steps,),
        in_specs=[pl.BlockSpec((lines, LANES), lambda g: (g, 0))] * 2
        + [pl.BlockSpec(w.shape, lambda g: (0, 0)) for w in weights],
        out_specs=[pl.BlockSpec((n_sets, 2, 2, cols, SUB, LANES), lambda g: (0, 0, 0, 0, g, 0))] * chunks,
        out_shape=[jax.ShapeDtypeStruct(shape, jnp.float32)] * chunks,
        scratch_shapes=[
            pltpu.VMEM((2, cols * SUB * pad, LANES), jnp.float32),
            pltpu.VMEM((2, cols * SUB * pad, LANES), jnp.float32),
            pltpu.VMEM((2, cols * SUB * pad, LANES), jnp.float32),
        ],
        compiler_params=pltpu.CompilerParams(vmem_limit_bytes=60 * 1024 * 1024),
        name="enter",
    )(x_real, x_imag, *weights)


def leave(sets, cav, rows, cols):
    dims = kernel_dims(cav, cols)
    _, _, _, pad, chunks = dims
    lines = cav * cols * cav // LANES * SUB
    steps = rows // SUB
    n_sets = 8
    return pl.pallas_call(
        functools.partial(leave_kernel, dims),
        grid=(steps,),
        in_specs=[pl.BlockSpec((n_sets, 2, 2, cols, SUB, LANES), lambda g: (0, 0, 0, 0, g, 0))] * chunks,
        out_specs=[pl.BlockSpec((lines, LANES), lambda g: (g, 0))] * 2,
        out_shape=[jax.ShapeDtypeStruct((lines * steps, LANES), jnp.float32)] * 2,
        scratch_shapes=[
            pltpu.VMEM((2, cols * SUB * pad, LANES), jnp.float32),
            pltpu.VMEM((2, cols * SUB * pad, LANES), jnp.float32),
        ],
        compiler_params=pltpu.CompilerParams(vmem_limit_bytes=60 * 1024 * 1024),
        name="leave",
    )(*sets)


def pair_tables(groups):
    uppers = [(i, j) for i in range(groups) for j in range(i + 1, groups)]
    diagonals = [(2 * i, 2 * i + 1) for i in range(groups // 2)]
    return uppers, diagonals


def ket_kernel(base, flags, own_ref, wh_ref, wl_ref, row_ref, ends_ref, mids_ref, corner_ref, sent_ref, half_ref):
    halves, cols, rows = base
    width = halves * cols
    own = own_ref[0, :] > 0

    @pl.when(flags[1] == 0)
    def _():
        far = flags[0]

        def own_row(block):
            spot = lax.select(far == 1, 3 - block, block)

            def by_bra(side, part, n):
                return row_ref[spot * halves + n // cols, side, part, n % cols]

            def by_ket(side, part, m):
                pieces = [
                    row_ref.at[spot * halves + h, side, part].reshape(cols * rows, LANES)[pl.ds(m, cols, stride=rows), :]
                    for h in range(halves)
                ]
                return jnp.concatenate(pieces, axis=0)

            return by_bra, by_ket

        def got(ref, lead):
            view = ref if lead is None else ref.at[lead]

            def by_bra(side, part, n):
                return view[n // cols, side, part, n % cols]

            def by_ket(side, part, m):
                pieces = [
                    view.at[h, side, part].reshape(cols * rows, LANES)[pl.ds(m, cols, stride=rows), :]
                    for h in range(halves)
                ]
                return jnp.concatenate(pieces, axis=0)

            return by_bra, by_ket

        known = {
            (1, 0): own_row(0),
            (1, 1): own_row(1),
            (1, 2): own_row(2),
            (1, 3): own_row(3),
            (0, 0): got(ends_ref, 0),
            (0, 2): got(ends_ref, 1),
            (0, 3): got(ends_ref, 2),
            (2, 3): got(mids_ref, 0),
            (2, 2): got(mids_ref, 1),
            (3, 3): got(corner_ref, None),
        }
        weights = (wh_ref[...], wl_ref[...])

        for block in range(4):

            def step(n, carry, block=block):
                columns = []
                for side in range(2):
                    pieces = []
                    for part in range(2):
                        for p in range(4):
                            if (p, block) in known:
                                pieces.append(known[p, block][0](side, part, n))
                            else:
                                read = known[block, p][1]
                                value = jnp.where(own, read(side, part, n), read(1 - side, part, n))
                                pieces.append(-value if part else value)
                    columns.append(jnp.concatenate(pieces, axis=0))
                result = dot3(weights, split_high(jnp.concatenate(columns, axis=1)))
                for side in range(2):
                    lanes = slice(side * LANES, (side + 1) * LANES)
                    for part in range(2):
                        top = part * 2 * rows
                        if block:
                            sent_ref[side, part, (block - 1) * width + n] = result[top : top + rows, lanes]
                        half_ref[side, part, block * width + n] = result[top + rows : top + 2 * rows, lanes]
                return carry

            lax.fori_loop(0, width, step, 0)


def bra_kernel(base, flags, own_ref, eh_ref, el_ref, bh_ref, bl_ref, row_ref, part_ref, half_ref, out_ref, work):
    halves, cols, rows = base
    width = halves * cols
    mech = 4 * width
    own = own_ref[0, :] > 0
    far = flags[0]

    def spot_of(block):
        return lax.select(far == 1, 3 - block, block)

    @pl.when(flags[1] == 1)
    def _():
        def by_ket(block, side, part, m):
            pieces = [
                row_ref.at[spot_of(block) * halves + h, side, part].reshape(cols * rows, LANES)[
                    pl.ds(m, cols, stride=rows), :
                ]
                for h in range(halves)
            ]
            return jnp.concatenate(pieces, axis=0)

        weights = (eh_ref[...], el_ref[...])

        for block in range(4):

            def step(n, carry, block=block):
                columns = []
                for side in range(2):
                    pieces = []
                    for part in range(2):
                        pieces.append(row_ref[spot_of(block) * halves + n // cols, side, part, n % cols])
                        for p in range(1, 4):
                            if block:
                                pieces.append(jnp.zeros((rows, LANES), jnp.float32))
                            else:
                                value = jnp.where(own, by_ket(p, side, part, n), by_ket(p, 1 - side, part, n))
                                pieces.append(-value if part else value)
                    columns.append(jnp.concatenate(pieces, axis=0))
                result = dot3(weights, split_high(jnp.concatenate(columns, axis=1)))
                for side in range(2):
                    for part in range(2):
                        value = result[part * rows : (part + 1) * rows, side * LANES : (side + 1) * LANES]
                        if block:
                            value = value + part_ref[side, part, (block - 1) * width + n]
                        work[side, part, pl.ds(pl.multiple_of((block * width + n) * rows, SUB), rows), :] = value
                return carry

            lax.fori_loop(0, width, step, 0)

    @pl.when(flags[1] == 0)
    def _():
        def step(n, carry):
            for side in range(2):
                for part in range(2):
                    work[side, part, pl.ds(pl.multiple_of(n * rows, SUB), rows), :] = half_ref[side, part, n]
            return carry

        lax.fori_loop(0, mech, step, 0)

    weights = (bh_ref[...], bl_ref[...])

    def finish(m, carry):
        columns = [
            jnp.concatenate([work[side, part, pl.ds(m, mech, stride=rows), :] for part in range(2)], axis=0)
            for side in range(2)
        ]
        result = dot3(weights, split_high(jnp.concatenate(columns, axis=1)))
        for side in range(2):
            for part in range(2):
                value = result[part * mech : (part + 1) * mech, side * LANES : (side + 1) * LANES]
                work[side, part, pl.ds(m, mech, stride=rows), :] = value
        return carry

    lax.fori_loop(0, rows, finish, 0)

    def put(q, carry):
        spot = lax.select(far == 1, 3 - q // width, q // width)
        for side in range(2):
            for part in range(2):
                value = work[side, part, pl.ds(pl.multiple_of(q * rows, SUB), rows), :]
                out_ref[spot * halves + q % width // cols, side, part, q % cols] = value
        return carry

    lax.fori_loop(0, mech, put, 0)


def whole_block(shape):
    return pl.BlockSpec(shape, lambda g, flags: (0,) * len(shape))


LIMIT = 48 * 1024 * 1024


def pick_blocks(got, flags):
    halves = got.shape[0] // 4
    far = flags[0] == 1

    def block_of(index):
        return lax.dynamic_slice_in_dim(got, jnp.where(far, 3 - index, index) * halves, halves, 0)

    return jnp.stack([block_of(0), block_of(2), block_of(3)]), jnp.stack([block_of(0), block_of(1)])


INNER = [(0, 1), (3, 2)]
CROSS = [(1, 2), (2, 1)]
BACK = [(1, 0), (2, 3)]


def mix_kets(got, ends, mids, corner, own, flags, weights):
    members, _, _, cols, rows, _ = got.shape
    halves = members // 4
    width = halves * cols
    args = (own, weights[0], weights[1], got, ends, mids, corner)
    shapes = ((2, 2, 3 * width, rows, LANES), (2, 2, 4 * width, rows, LANES))
    sent, half = pl.pallas_call(
        functools.partial(ket_kernel, (halves, cols, rows)),
        grid_spec=pltpu.PrefetchScalarGridSpec(
            num_scalar_prefetch=1,
            grid=(1,),
            in_specs=[whole_block(a.shape) for a in args],
            out_specs=[whole_block(shape) for shape in shapes],
        ),
        out_shape=[jax.ShapeDtypeStruct(shape, jnp.float32) for shape in shapes],
        compiler_params=pltpu.CompilerParams(vmem_limit_bytes=LIMIT),
        cost_estimate=pl.CostEstimate(flops=12_000_000_000, bytes_accessed=40_000_000, transcendentals=0),
        name="ket",
    )(flags, *args)
    return sent, half


def mix_bras(got, partial, half, own, flags, end_line, bra):
    members, _, _, cols, rows, _ = got.shape
    halves = members // 4
    args = (own, end_line[0], end_line[1], bra[0], bra[1], got, partial, half)
    return pl.pallas_call(
        functools.partial(bra_kernel, (halves, cols, rows)),
        grid_spec=pltpu.PrefetchScalarGridSpec(
            num_scalar_prefetch=1,
            grid=(1,),
            in_specs=[whole_block(a.shape) for a in args],
            out_specs=whole_block(got.shape),
            scratch_shapes=[pltpu.VMEM((2, 2, members * cols * rows, LANES), jnp.float32)],
        ),
        out_shape=jax.ShapeDtypeStruct(got.shape, jnp.float32),
        compiler_params=pltpu.CompilerParams(vmem_limit_bytes=LIMIT),
        cost_estimate=pl.CostEstimate(flops=12_000_000_000, bytes_accessed=40_000_000, transcendentals=0),
        name="bra",
    )(flags, *args)


def swap_plane(array):
    return lax.all_to_all(array, "col", split_axis=0, concat_axis=0, tiled=True)


def realified(real_part, imag_part, sign):
    top = jnp.concatenate([real_part, -sign * imag_part], axis=1)
    bottom = jnp.concatenate([sign * imag_part, real_part], axis=1)
    return split_weights(jnp.concatenate([top, bottom], axis=0))


def fast_local(rho_real, rho_imag, cav_real, cav_imag, mech_real, mech_imag):
    block_shape = rho_real.shape
    cav = cav_real.shape[0]
    mech = mech_real.shape[0]
    n_row, n_col = lax.axis_size("row"), lax.axis_size("col")
    rows, cols = mech // n_row, mech // n_col
    size = cav // n_row
    sets = enter(
        rho_real.reshape(-1, LANES), rho_imag.reshape(-1, LANES), cav_real, cav_imag, rows, cols
    )
    chunks = len(sets)

    place = lax.axis_index("row")
    member = lax.axis_index("col")
    far_half = place >= n_row // 2
    is_end = (place == 0) | (place == n_row - 1)
    flags = jnp.stack([far_half, is_end]).astype(jnp.int32)
    lanes = jnp.arange(chunks * LANES)
    uppers, _ = pair_tables(n_row)
    own_lanes = ((member >= len(uppers)) & ((lanes // size) == (lanes % size))).astype(jnp.int32)

    def order(matrix):
        shaped = matrix.reshape(n_row, rows, n_row, rows)
        return jnp.where(far_half, shaped[::-1, :, ::-1], shaped).reshape(mech, mech)

    mixer_real, mixer_imag = order(mech_real), order(mech_imag)
    outside = (jnp.arange(mech) >= rows)[None, :]
    away_real = jnp.where(outside, mixer_real[:rows], 0.0)
    away_imag = jnp.where(outside, mixer_imag[:rows], 0.0)
    whole = realified(
        jnp.concatenate([away_real, mixer_real[rows : 2 * rows]]),
        jnp.concatenate([away_imag, mixer_imag[rows : 2 * rows]]),
        1.0,
    )
    end_line = realified(mixer_real[:rows], mixer_imag[:rows], 1.0)
    bra = realified(mixer_real, mixer_imag, -1.0)
    own = [own_lanes[chunk * LANES : (chunk + 1) * LANES][None] for chunk in range(chunks)]

    state = {("set", chunk): sets[chunk] for chunk in range(chunks)}

    def settle(made):
        state.update(made)
        names = sorted(state)
        state.update(zip(names, lax.optimization_barrier([state[name] for name in names])))

    for tick in range(chunks + 3):
        fresh, moved, mixed, last = (tick - back for back in range(4))
        made = {}
        if fresh < chunks:
            made["row", fresh] = swap_plane(state.pop(("set", fresh)))
        if 0 <= moved < chunks:
            ends, mids = state.pop(("pick", moved))
            made["ends", moved] = lax.ppermute(ends, "row", INNER)
            made["mids", moved] = lax.ppermute(mids, "row", CROSS)
        if 0 <= mixed < chunks:
            parts = [state.pop((name, mixed)) for name in ("ends", "mids", "corner")]
            made["half", mixed] = mix_kets(state["row", mixed], *parts, own[mixed], flags, whole)
        if 0 <= last < chunks:
            parts = [state.pop((name, last)) for name in ("row", "partial", "mine")]
            made["out", last] = mix_bras(*parts, own[last], flags, end_line, bra)
        settle(made)
        made = {}
        if fresh < chunks:
            made["pick", fresh] = pick_blocks(state["row", fresh], flags)
        if 0 <= moved < chunks:
            made["corner", moved] = lax.ppermute(state["ends", moved][0], "row", CROSS)
        if 0 <= mixed < chunks:
            sent, made["mine", mixed] = state.pop(("half", mixed))
            made["partial", mixed] = lax.ppermute(sent, "row", BACK)
        if 0 <= last < chunks:
            made["done", last] = swap_plane(state.pop(("out", last)))
        settle(made)
    results = [state["done", chunk] for chunk in range(chunks)]
    final = leave(results, cav, rows, cols)
    return final[0].reshape(block_shape), final[1].reshape(block_shape)


def fits(mesh, mech, cav):
    n_row, n_col = mesh.shape["row"], mesh.shape["col"]
    if n_row != 4 or n_col != 2 * n_row or mech % n_col:
        return False
    return kernels_fit(mech // n_row, mech // n_col, cav)


def solution(mesh):
    def whole(rho_real, rho_imag, cav_real, cav_imag, mech_real, mech_imag):
        local = fast_local if fits(mesh, mech_real.shape[0], cav_real.shape[0]) else general_local
        return jax.shard_map(
            local,
            mesh=mesh,
            in_specs=(P("row", "col", None), P("row", "col", None), P(), P(), P(), P()),
            out_specs=(P("row", "col", None), P("row", "col", None)),
            check_vma=False,
        )(rho_real, rho_imag, cav_real, cav_imag, mech_real, mech_imag)

    return whole
```

```python
import functools
import math

import jax
import jax.numpy as jnp
from jax import lax
from jax.experimental import pallas as pl
from jax.experimental.pallas import tpu as pltpu
from jax.sharding import PartitionSpec as P

highest = lax.Precision.HIGHEST


def cavity_sides(parts, cav_real, cav_imag):
    real_part, imag_part = parts
    left_real = jnp.einsum("cd,mdne->mcne", cav_real, real_part, precision=highest) - jnp.einsum(
        "cd,mdne->mcne", cav_imag, imag_part, precision=highest
    )
    left_imag = jnp.einsum("cd,mdne->mcne", cav_real, imag_part, precision=highest) + jnp.einsum(
        "cd,mdne->mcne", cav_imag, real_part, precision=highest
    )
    right_real = jnp.einsum("mcne,fe->mcnf", left_real, cav_real, precision=highest) + jnp.einsum(
        "mcne,fe->mcnf", left_imag, cav_imag, precision=highest
    )
    right_imag = jnp.einsum("mcne,fe->mcnf", left_imag, cav_real, precision=highest) - jnp.einsum(
        "mcne,fe->mcnf", left_real, cav_imag, precision=highest
    )
    return (right_real, right_imag)


def mech_mix(pieces, mech_real, mech_imag, adjoint):
    real_part, imag_part = pieces
    plain_rr = jnp.einsum("mn,nok->mok", mech_real, real_part, precision=highest)
    plain_ii = jnp.einsum("mn,nok->mok", mech_imag, imag_part, precision=highest)
    plain_ri = jnp.einsum("mn,nok->mok", mech_real, imag_part, precision=highest)
    plain_ir = jnp.einsum("mn,nok->mok", mech_imag, real_part, precision=highest)
    if adjoint:
        return (plain_rr + plain_ii, plain_ri - plain_ir)
    return (plain_rr - plain_ii, plain_ri + plain_ir)


def ket_side(parts, mech_real, mech_imag):
    real_part, imag_part = parts
    local_rows, cav_count, local_cols, width = real_part.shape
    groups = lax.axis_size("row")
    flat = cav_count * local_cols * width
    shaped = (
        real_part.reshape(local_rows, groups, flat // groups),
        imag_part.reshape(local_rows, groups, flat // groups),
    )
    mixed = mech_mix(
        (
            lax.all_to_all(shaped[0], "row", split_axis=1, concat_axis=0, tiled=True),
            lax.all_to_all(shaped[1], "row", split_axis=1, concat_axis=0, tiled=True),
        ),
        mech_real,
        mech_imag,
        False,
    )
    return (
        lax.all_to_all(mixed[0], "row", split_axis=0, concat_axis=1, tiled=True).reshape(
            local_rows, cav_count, local_cols, width
        ),
        lax.all_to_all(mixed[1], "row", split_axis=0, concat_axis=1, tiled=True).reshape(
            local_rows, cav_count, local_cols, width
        ),
    )


def bra_side(parts, mech_real, mech_imag):
    real_part, imag_part = parts
    local_rows, cav_count, local_cols, width = real_part.shape
    groups = lax.axis_size("col")
    flat = local_rows * cav_count * width
    moved_real = jnp.transpose(real_part, (2, 0, 1, 3)).reshape(local_cols, groups, flat // groups)
    moved_imag = jnp.transpose(imag_part, (2, 0, 1, 3)).reshape(local_cols, groups, flat // groups)
    mixed = mech_mix(
        (
            lax.all_to_all(moved_real, "col", split_axis=1, concat_axis=0, tiled=True),
            lax.all_to_all(moved_imag, "col", split_axis=1, concat_axis=0, tiled=True),
        ),
        mech_real,
        mech_imag,
        True,
    )
    back_real = jnp.transpose(
        lax.all_to_all(mixed[0], "col", split_axis=0, concat_axis=1, tiled=True).reshape(
            local_cols, local_rows, cav_count, width
        ),
        (1, 2, 0, 3),
    )
    back_imag = jnp.transpose(
        lax.all_to_all(mixed[1], "col", split_axis=0, concat_axis=1, tiled=True).reshape(
            local_cols, local_rows, cav_count, width
        ),
        (1, 2, 0, 3),
    )
    return (back_real, back_imag)


def general_local(rho_real, rho_imag, cav_real, cav_imag, mech_real, mech_imag):
    block_shape = rho_real.shape
    cav_count = cav_real.shape[0]
    local_rows = mech_real.shape[0] // lax.axis_size("row")
    local_cols = mech_real.shape[0] // lax.axis_size("col")
    shape_four = (local_rows, cav_count, local_cols, cav_count)
    state = (rho_real.reshape(shape_four), rho_imag.reshape(shape_four))
    state = cavity_sides(state, cav_real, cav_imag)
    state = bra_side(ket_side(state, mech_real, mech_imag), mech_real, mech_imag)
    return (state[0].reshape(block_shape), state[1].reshape(block_shape))


LANES = 128
SUB = 8


def set_pieces(groups, size):
    uppers, diagonals = pair_tables(groups)
    table = []
    for i, j in uppers:
        rows = [[(size * k, size * i + k, size * j)] for k in range(size)]
        table.append((rows, rows))
    for i, j in diagonals:
        first, second = [], []
        for k in range(size):
            low, high = (size * k, size * j + k, size * j), (size * i + k, size * i)
            first.append(([low] if k else []) + [(size * k + k,) + (high[0], high[1] + k)])
            upper = [(size * k + k + 1, high[0], high[1] + k + 1)] if k + 1 < size else []
            second.append([low] + upper)
        table.append((first, second))
    return table


def split_high(value):
    high = value.astype(jnp.bfloat16)
    return high, (value - high.astype(jnp.float32)).astype(jnp.bfloat16)


def split_weights(value):
    high = lax.reduce_precision(value, exponent_bits=8, mantissa_bits=7)
    return high.astype(jnp.bfloat16), (value - high).astype(jnp.bfloat16)


def dot3(left, right):
    total = jnp.dot(left[0], right[1], preferred_element_type=jnp.float32)
    total += jnp.dot(left[1], right[0], preferred_element_type=jnp.float32)
    return total + jnp.dot(left[0], right[0], preferred_element_type=jnp.float32)


def row_span(cols):
    return SUB * (cols + 1 - cols % 2)


def lane_index():
    return lax.broadcasted_iota(jnp.int32, (SUB, LANES), 1)


def turn(value, shift):
    return pltpu.roll(value, shift % LANES, 1) if shift % LANES else value


def enter_kernel(dims, *refs):
    cav, cols, period, pad, chunks = dims
    x_refs, (lh, ll, rh, rl) = refs[:2], refs[2:6]
    outs = refs[6 : 6 + chunks]
    work, plain, turned = refs[6 + chunks :]
    lane = lane_index()
    stride = x_refs[0].shape[0] // SUB
    step_rows = period * cols * cav // LANES
    count = cols * SUB
    span = row_span(cols)

    @pl.when(pl.program_id(0) == 0)
    def _():
        work[...] = jnp.zeros_like(work)

    def unroll(outer, carry):
        for part in range(2):
            for inner in range(period):
                for col in range(cols):
                    place = (inner * cols + col) * cav
                    row, shift = outer * step_rows + place // LANES, place % LANES
                    value = x_refs[part][pl.ds(row, SUB, stride=stride), :]
                    if shift + cav > LANES:
                        after = x_refs[part][pl.ds(row + 1, SUB, stride=stride), :]
                        value = jnp.where(lane >= shift, value, after)
                    target = col * SUB * pad + outer * period + inner
                    work[part, pl.ds(target, SUB, stride=pad), :] = turn(value, -shift)
        return carry

    lax.fori_loop(0, cav // period, unroll, 0)

    left = (lh[...], ll[...])
    right = (rh[...], rl[...])

    def mix(pair, carry):
        halves = []
        for extra in range(2):
            start = pl.multiple_of((2 * pair + extra) * pad, SUB)
            halves.append(jnp.concatenate([work[0, pl.ds(start, pad), :], work[1, pl.ds(start, pad), :]], axis=0))
        ket = dot3(left, split_high(jnp.concatenate(halves, axis=1)))
        stacked = jnp.concatenate(
            [
                jnp.concatenate([ket[:pad, lo : lo + LANES], ket[LANES : LANES + pad, lo : lo + LANES]], axis=1)
                for lo in (0, LANES)
            ],
            axis=0,
        )
        both = dot3(split_high(stacked), right)
        for extra in range(2):
            for part in range(2):
                block = both[extra * pad : (extra + 1) * pad, part * LANES : (part + 1) * LANES]
                plain[part, pl.ds(2 * pair + extra, pad, stride=span), :] = block
                square = jnp.concatenate([block, jnp.zeros((LANES - pad, LANES), jnp.float32)], axis=0)
                turned[part, pl.ds(2 * pair + extra, pad, stride=span), :] = jnp.transpose(square)[:pad]
        return carry

    lax.fori_loop(0, count // 2, mix, 0)

    size = cav // 4
    table = set_pieces(4, size)
    end = size * size

    def gather(col, carry):
        for chunk in range(chunks):
            base = chunk * LANES
            for index, pair in enumerate(table):
                for side in range(2):
                    source = (plain, turned)[side]
                    pieces = [piece for row in pair[side] for piece in row]
                    for part in range(2):
                        total = None
                        for at, (first, row, lane_from) in enumerate(pieces):
                            last = pieces[at + 1][0] if at + 1 < len(pieces) else end
                            if last <= base or first >= base + LANES:
                                continue
                            start = pl.multiple_of(row * span + col * SUB, SUB)
                            value = turn(source[part, pl.ds(start, SUB), :], first - base - lane_from)
                            total = value if total is None else jnp.where(lane >= first - base, value, total)
                        if end < base + LANES:
                            total = jnp.where(lane < end - base, total, 0.0)
                        outs[chunk][index, side, part, col] = total
        return carry

    lax.fori_loop(0, cols, gather, 0)


def leave_kernel(dims, *refs):
    cav, cols, period, pad, chunks = dims
    ins, outs = refs[:chunks], refs[chunks : chunks + 2]
    plain, turned = refs[chunks + 2 :]
    lane = lane_index()
    count = cols * SUB
    span = row_span(cols)
    size = cav // 4
    groups = 4
    table = set_pieces(groups, size)
    end = size * size

    def scatter(col, carry):
        for side in range(2):
            target = (plain, turned)[side]
            found = [[] for _ in range(cav)]
            for index, pair in enumerate(table):
                pieces = [piece for row in pair[side] for piece in row]
                for at, (first, row, lane_from) in enumerate(pieces):
                    last = pieces[at + 1][0] if at + 1 < len(pieces) else end
                    while first < last:
                        stop = min(last, (first // LANES + 1) * LANES)
                        found[row].append((lane_from, stop - first, index, first))
                        lane_from, first = lane_from + stop - first, stop
            for row in range(cav):
                for part in range(2):
                    total, reach = None, 0
                    for lane_to, length, index, first in sorted(found[row]):
                        if total is None:
                            total = jnp.zeros((SUB, LANES), jnp.float32)
                        elif lane_to > reach:
                            total = jnp.where(lane >= reach, 0.0, total)
                        value = turn(ins[first // LANES][index, side, part, col], lane_to - first % LANES)
                        total = jnp.where(lane >= lane_to, value, total)
                        reach = lane_to + length
                    if total is None:
                        total = jnp.zeros((SUB, LANES), jnp.float32)
                    else:
                        total = jnp.where(lane < reach, total, 0.0)
                    start = pl.multiple_of(row * span + col * SUB, SUB)
                    target[part, pl.ds(start, SUB), :] = total
        return carry

    lax.fori_loop(0, cols, scatter, 0)

    def merge(index, carry):
        for part in range(2):
            block = turned[part, pl.ds(index, pad, stride=span), :]
            square = jnp.concatenate([block, jnp.zeros((LANES - pad, LANES), jnp.float32)], axis=0)
            rows = pl.ds(index, pad, stride=span)
            plain[part, rows, :] = plain[part, rows, :] + jnp.transpose(square)[:pad]
        return carry

    lax.fori_loop(0, count, merge, 0)

    stride = outs[0].shape[0] // SUB
    step_rows = period * cols * cav // LANES

    def store(outer, carry):
        for part in range(2):
            for inner in range(step_rows):
                begin = inner * LANES
                total = None
                for piece in range(begin // cav, (begin + LANES - 1) // cav + 1):
                    row = (outer * period + piece // cols) * span + (piece % cols) * SUB
                    value = turn(plain[part, pl.ds(pl.multiple_of(row, SUB), SUB), :], piece * cav - begin)
                    total = value if total is None else jnp.where(lane >= piece * cav - begin, value, total)
                outs[part][pl.ds(outer * step_rows + inner, SUB, stride=stride), :] = total
        return carry

    lax.fori_loop(0, cav // period, store, 0)


def kernel_dims(cav, cols):
    period = LANES // math.gcd(cols * cav, LANES)
    pad = -(-cav // SUB) * SUB
    chunks = -(-(cav // 4) ** 2 // LANES)
    return cav, cols, period, pad, chunks


def kernels_fit(rows, cols, cav):
    period = LANES // math.gcd(cols * cav, LANES)
    return rows % SUB == 0 and cols % 2 == 0 and cav % 4 == 0 and cav % period == 0 and 4 * SUB <= cav <= LANES


def enter(x_real, x_imag, cav_real, cav_imag, rows, cols):
    cav = cav_real.shape[0]
    dims = kernel_dims(cav, cols)
    _, _, _, pad, chunks = dims
    lines = cav * cols * cav // LANES * SUB
    steps = rows // SUB

    def put(matrix, height, width):
        return jnp.pad(matrix, ((0, height - cav), (0, width - cav)))

    ket = jnp.block(
        [
            [put(cav_real, LANES, pad), put(-cav_imag, LANES, pad)],
            [put(cav_imag, LANES, pad), put(cav_real, LANES, pad)],
        ]
    )
    bra = jnp.block(
        [
            [put(cav_real.T, LANES, LANES), put(-cav_imag.T, LANES, LANES)],
            [put(cav_imag.T, LANES, LANES), put(cav_real.T, LANES, LANES)],
        ]
    )
    weights = split_weights(ket) + split_weights(bra)
    n_sets = 8
    shape = (n_sets, 2, 2, cols, rows, LANES)
    return pl.pallas_call(
        functools.partial(enter_kernel, dims),
        grid=(steps,),
        in_specs=[pl.BlockSpec((lines, LANES), lambda g: (g, 0))] * 2
        + [pl.BlockSpec(w.shape, lambda g: (0, 0)) for w in weights],
        out_specs=[pl.BlockSpec((n_sets, 2, 2, cols, SUB, LANES), lambda g: (0, 0, 0, 0, g, 0))] * chunks,
        out_shape=[jax.ShapeDtypeStruct(shape, jnp.float32)] * chunks,
        scratch_shapes=[
            pltpu.VMEM((2, cols * SUB * pad, LANES), jnp.float32),
            pltpu.VMEM((2, row_span(cols) * pad, LANES), jnp.float32),
            pltpu.VMEM((2, row_span(cols) * pad, LANES), jnp.float32),
        ],
        compiler_params=pltpu.CompilerParams(vmem_limit_bytes=60 * 1024 * 1024),
        name="enter",
    )(x_real, x_imag, *weights)


def leave(sets, cav, rows, cols):
    dims = kernel_dims(cav, cols)
    _, _, _, pad, chunks = dims
    lines = cav * cols * cav // LANES * SUB
    steps = rows // SUB
    n_sets = 8
    return pl.pallas_call(
        functools.partial(leave_kernel, dims),
        grid=(steps,),
        in_specs=[pl.BlockSpec((n_sets, 2, 2, cols, SUB, LANES), lambda g: (0, 0, 0, 0, g, 0))] * chunks,
        out_specs=[pl.BlockSpec((lines, LANES), lambda g: (g, 0))] * 2,
        out_shape=[jax.ShapeDtypeStruct((lines * steps, LANES), jnp.float32)] * 2,
        scratch_shapes=[
            pltpu.VMEM((2, row_span(cols) * pad, LANES), jnp.float32),
            pltpu.VMEM((2, row_span(cols) * pad, LANES), jnp.float32),
        ],
        compiler_params=pltpu.CompilerParams(vmem_limit_bytes=60 * 1024 * 1024),
        name="leave",
    )(*sets)


def pair_tables(groups):
    uppers = [(i, j) for i in range(groups) for j in range(i + 1, groups)]
    diagonals = [(2 * i, 2 * i + 1) for i in range(groups // 2)]
    return uppers, diagonals


def ket_kernel(base, flags, own_ref, wh_ref, wl_ref, row_ref, ends_ref, mids_ref, corner_ref, sent_ref, half_ref):
    halves, cols, rows = base
    width = halves * cols
    own = own_ref[0, :] > 0

    @pl.when(flags[1] == 0)
    def _():
        far = flags[0]

        def own_row(block):
            spot = lax.select(far == 1, 3 - block, block)

            def by_bra(side, part, n):
                return row_ref[spot * halves + n // cols, side, part, n % cols]

            def by_ket(side, part, m):
                pieces = [
                    row_ref.at[spot * halves + h, side, part].reshape(cols * rows, LANES)[pl.ds(m, cols, stride=rows), :]
                    for h in range(halves)
                ]
                return jnp.concatenate(pieces, axis=0)

            return by_bra, by_ket

        def got(ref, lead):
            view = ref if lead is None else ref.at[lead]

            def by_bra(side, part, n):
                return view[n // cols, side, part, n % cols]

            def by_ket(side, part, m):
                pieces = [
                    view.at[h, side, part].reshape(cols * rows, LANES)[pl.ds(m, cols, stride=rows), :]
                    for h in range(halves)
                ]
                return jnp.concatenate(pieces, axis=0)

            return by_bra, by_ket

        known = {
            (1, 0): own_row(0),
            (1, 1): own_row(1),
            (1, 2): own_row(2),
            (1, 3): own_row(3),
            (0, 0): got(ends_ref, 0),
            (0, 2): got(ends_ref, 1),
            (0, 3): got(ends_ref, 2),
            (2, 3): got(mids_ref, 0),
            (2, 2): got(mids_ref, 1),
            (3, 3): got(corner_ref, None),
        }
        weights = (wh_ref[...], wl_ref[...])

        for block in range(4):

            def step(n, carry, block=block):
                columns = []
                for side in range(2):
                    pieces = []
                    for part in range(2):
                        for p in range(4):
                            if (p, block) in known:
                                pieces.append(known[p, block][0](side, part, n))
                            else:
                                read = known[block, p][1]
                                value = jnp.where(own, read(side, part, n), read(1 - side, part, n))
                                pieces.append(-value if part else value)
                    columns.append(jnp.concatenate(pieces, axis=0))
                result = dot3(weights, split_high(jnp.concatenate(columns, axis=1)))
                for side in range(2):
                    lanes = slice(side * LANES, (side + 1) * LANES)
                    for part in range(2):
                        top = part * 2 * rows
                        if block:
                            sent_ref[side, part, (block - 1) * width + n] = result[top : top + rows, lanes]
                        half_ref[side, part, block * width + n] = result[top + rows : top + 2 * rows, lanes]
                return carry

            lax.fori_loop(0, width, step, 0)


def bra_kernel(base, flags, own_ref, eh_ref, el_ref, bh_ref, bl_ref, row_ref, part_ref, half_ref, out_ref, work):
    halves, cols, rows = base
    width = halves * cols
    mech = 4 * width
    span = row_span(rows // SUB)
    own = own_ref[0, :] > 0
    far = flags[0]

    def spot_of(block):
        return lax.select(far == 1, 3 - block, block)

    @pl.when(flags[1] == 1)
    def _():
        def by_ket(block, side, part, m):
            pieces = [
                row_ref.at[spot_of(block) * halves + h, side, part].reshape(cols * rows, LANES)[
                    pl.ds(m, cols, stride=rows), :
                ]
                for h in range(halves)
            ]
            return jnp.concatenate(pieces, axis=0)

        weights = (eh_ref[...], el_ref[...])

        for block in range(4):

            def step(n, carry, block=block):
                columns = []
                for side in range(2):
                    pieces = []
                    for part in range(2):
                        pieces.append(row_ref[spot_of(block) * halves + n // cols, side, part, n % cols])
                        for p in range(1, 4):
                            if block:
                                pieces.append(jnp.zeros((rows, LANES), jnp.float32))
                            else:
                                value = jnp.where(own, by_ket(p, side, part, n), by_ket(p, 1 - side, part, n))
                                pieces.append(-value if part else value)
                    columns.append(jnp.concatenate(pieces, axis=0))
                result = dot3(weights, split_high(jnp.concatenate(columns, axis=1)))
                for side in range(2):
                    for part in range(2):
                        value = result[part * rows : (part + 1) * rows, side * LANES : (side + 1) * LANES]
                        if block:
                            value = value + part_ref[side, part, (block - 1) * width + n]
                        work[side, part, pl.ds(pl.multiple_of((block * width + n) * span, SUB), rows), :] = value
                return carry

            lax.fori_loop(0, width, step, 0)

    @pl.when(flags[1] == 0)
    def _():
        def step(n, carry):
            for side in range(2):
                for part in range(2):
                    work[side, part, pl.ds(pl.multiple_of(n * span, SUB), rows), :] = half_ref[side, part, n]
            return carry

        lax.fori_loop(0, mech, step, 0)

    weights = (bh_ref[...], bl_ref[...])

    def finish(m, carry):
        columns = [
            jnp.concatenate([work[side, part, pl.ds(m, mech, stride=span), :] for part in range(2)], axis=0)
            for side in range(2)
        ]
        result = dot3(weights, split_high(jnp.concatenate(columns, axis=1)))
        for side in range(2):
            for part in range(2):
                value = result[part * mech : (part + 1) * mech, side * LANES : (side + 1) * LANES]
                work[side, part, pl.ds(m, mech, stride=span), :] = value
        return carry

    lax.fori_loop(0, rows, finish, 0)

    def put(q, carry):
        spot = lax.select(far == 1, 3 - q // width, q // width)
        for side in range(2):
            for part in range(2):
                value = work[side, part, pl.ds(pl.multiple_of(q * span, SUB), rows), :]
                out_ref[spot * halves + q % width // cols, side, part, q % cols] = value
        return carry

    lax.fori_loop(0, mech, put, 0)


def whole_block(shape):
    return pl.BlockSpec(shape, lambda g, flags: (0,) * len(shape))


LIMIT = 48 * 1024 * 1024


def pick_blocks(got, flags):
    halves = got.shape[0] // 4
    far = flags[0] == 1

    def block_of(index):
        return lax.dynamic_slice_in_dim(got, jnp.where(far, 3 - index, index) * halves, halves, 0)

    return jnp.stack([block_of(0), block_of(2), block_of(3)]), jnp.stack([block_of(0), block_of(1)])


INNER = [(0, 1), (3, 2)]
CROSS = [(1, 2), (2, 1)]
BACK = [(1, 0), (2, 3)]


def mix_kets(got, ends, mids, corner, own, flags, weights):
    members, _, _, cols, rows, _ = got.shape
    halves = members // 4
    width = halves * cols
    args = (own, weights[0], weights[1], got, ends, mids, corner)
    shapes = ((2, 2, 3 * width, rows, LANES), (2, 2, 4 * width, rows, LANES))
    sent, half = pl.pallas_call(
        functools.partial(ket_kernel, (halves, cols, rows)),
        grid_spec=pltpu.PrefetchScalarGridSpec(
            num_scalar_prefetch=1,
            grid=(1,),
            in_specs=[whole_block(a.shape) for a in args],
            out_specs=[whole_block(shape) for shape in shapes],
        ),
        out_shape=[jax.ShapeDtypeStruct(shape, jnp.float32) for shape in shapes],
        compiler_params=pltpu.CompilerParams(vmem_limit_bytes=LIMIT),
        cost_estimate=pl.CostEstimate(flops=12_000_000_000, bytes_accessed=40_000_000, transcendentals=0),
        name="ket",
    )(flags, *args)
    return sent, half


def mix_bras(got, partial, half, own, flags, end_line, bra):
    members, _, _, cols, rows, _ = got.shape
    halves = members // 4
    args = (own, end_line[0], end_line[1], bra[0], bra[1], got, partial, half)
    return pl.pallas_call(
        functools.partial(bra_kernel, (halves, cols, rows)),
        grid_spec=pltpu.PrefetchScalarGridSpec(
            num_scalar_prefetch=1,
            grid=(1,),
            in_specs=[whole_block(a.shape) for a in args],
            out_specs=whole_block(got.shape),
            scratch_shapes=[pltpu.VMEM((2, 2, members * cols * row_span(rows // SUB), LANES), jnp.float32)],
        ),
        out_shape=jax.ShapeDtypeStruct(got.shape, jnp.float32),
        compiler_params=pltpu.CompilerParams(vmem_limit_bytes=LIMIT),
        cost_estimate=pl.CostEstimate(flops=12_000_000_000, bytes_accessed=40_000_000, transcendentals=0),
        name="bra",
    )(flags, *args)


def swap_plane(array):
    return lax.all_to_all(array, "col", split_axis=0, concat_axis=0, tiled=True)


def realified(real_part, imag_part, sign):
    top = jnp.concatenate([real_part, -sign * imag_part], axis=1)
    bottom = jnp.concatenate([sign * imag_part, real_part], axis=1)
    return split_weights(jnp.concatenate([top, bottom], axis=0))


def fast_local(rho_real, rho_imag, cav_real, cav_imag, mech_real, mech_imag):
    block_shape = rho_real.shape
    cav = cav_real.shape[0]
    mech = mech_real.shape[0]
    n_row, n_col = lax.axis_size("row"), lax.axis_size("col")
    rows, cols = mech // n_row, mech // n_col
    size = cav // n_row
    sets = enter(
        rho_real.reshape(-1, LANES), rho_imag.reshape(-1, LANES), cav_real, cav_imag, rows, cols
    )
    chunks = len(sets)

    place = lax.axis_index("row")
    member = lax.axis_index("col")
    far_half = place >= n_row // 2
    is_end = (place == 0) | (place == n_row - 1)
    flags = jnp.stack([far_half, is_end]).astype(jnp.int32)
    lanes = jnp.arange(chunks * LANES)
    uppers, _ = pair_tables(n_row)
    own_lanes = ((member >= len(uppers)) & ((lanes // size) == (lanes % size))).astype(jnp.int32)

    def order(matrix):
        shaped = matrix.reshape(n_row, rows, n_row, rows)
        return jnp.where(far_half, shaped[::-1, :, ::-1], shaped).reshape(mech, mech)

    mixer_real, mixer_imag = order(mech_real), order(mech_imag)
    outside = (jnp.arange(mech) >= rows)[None, :]
    away_real = jnp.where(outside, mixer_real[:rows], 0.0)
    away_imag = jnp.where(outside, mixer_imag[:rows], 0.0)
    whole = realified(
        jnp.concatenate([away_real, mixer_real[rows : 2 * rows]]),
        jnp.concatenate([away_imag, mixer_imag[rows : 2 * rows]]),
        1.0,
    )
    end_line = realified(mixer_real[:rows], mixer_imag[:rows], 1.0)
    bra = realified(mixer_real, mixer_imag, -1.0)
    own = [own_lanes[chunk * LANES : (chunk + 1) * LANES][None] for chunk in range(chunks)]

    state = {("set", chunk): sets[chunk] for chunk in range(chunks)}
    for tick in range(chunks + 5):
        fresh, moved, mixed, sent, last, gone = (tick - back for back in range(6))
        made = {}
        if fresh < chunks:
            made["row", fresh] = swap_plane(state.pop(("set", fresh)))
        if 0 <= gone < chunks:
            made["done", gone] = swap_plane(state.pop(("out", gone)))
        if 0 <= moved < chunks:
            ends, mids = pick_blocks(state["row", moved], flags)
            made["ends", moved] = lax.ppermute(ends, "row", INNER)
            made["mids", moved] = lax.ppermute(mids, "row", CROSS)
        if 0 <= sent < chunks:
            made["partial", sent] = lax.ppermute(state.pop(("sent", sent)), "row", BACK)
        if 0 <= mixed < chunks:
            ends, mids = state.pop(("ends", mixed)), state.pop(("mids", mixed))
            corner = lax.ppermute(ends[0], "row", CROSS)
            made["sent", mixed], made["mine", mixed] = mix_kets(
                state["row", mixed], ends, mids, corner, own[mixed], flags, whole
            )
        if 0 <= last < chunks:
            parts = [state.pop((name, last)) for name in ("row", "partial", "mine")]
            made["out", last] = mix_bras(*parts, own[last], flags, end_line, bra)
        state.update(made)
        names = sorted(state)
        state.update(zip(names, lax.optimization_barrier([state[name] for name in names])))
    results = [state["done", chunk] for chunk in range(chunks)]
    final = leave(results, cav, rows, cols)
    return final[0].reshape(block_shape), final[1].reshape(block_shape)


def fits(mesh, mech, cav):
    n_row, n_col = mesh.shape["row"], mesh.shape["col"]
    if n_row != 4 or n_col != 2 * n_row or mech % n_col:
        return False
    return kernels_fit(mech // n_row, mech // n_col, cav)


def solution(mesh):
    def whole(rho_real, rho_imag, cav_real, cav_imag, mech_real, mech_imag):
        local = fast_local if fits(mesh, mech_real.shape[0], cav_real.shape[0]) else general_local
        return jax.shard_map(
            local,
            mesh=mesh,
            in_specs=(P("row", "col", None), P("row", "col", None), P(), P(), P(), P()),
            out_specs=(P("row", "col", None), P("row", "col", None)),
            check_vma=False,
        )(rho_real, rho_imag, cav_real, cav_imag, mech_real, mech_imag)

    return whole
```

```python
import functools
import math

import jax
import jax.numpy as jnp
from jax import lax
from jax.experimental import pallas as pl
from jax.experimental.pallas import tpu as pltpu
from jax.sharding import PartitionSpec as P

highest = lax.Precision.HIGHEST


def cavity_sides(parts, cav_real, cav_imag):
    real_part, imag_part = parts
    left_real = jnp.einsum("cd,mdne->mcne", cav_real, real_part, precision=highest) - jnp.einsum(
        "cd,mdne->mcne", cav_imag, imag_part, precision=highest
    )
    left_imag = jnp.einsum("cd,mdne->mcne", cav_real, imag_part, precision=highest) + jnp.einsum(
        "cd,mdne->mcne", cav_imag, real_part, precision=highest
    )
    right_real = jnp.einsum("mcne,fe->mcnf", left_real, cav_real, precision=highest) + jnp.einsum(
        "mcne,fe->mcnf", left_imag, cav_imag, precision=highest
    )
    right_imag = jnp.einsum("mcne,fe->mcnf", left_imag, cav_real, precision=highest) - jnp.einsum(
        "mcne,fe->mcnf", left_real, cav_imag, precision=highest
    )
    return (right_real, right_imag)


def mech_mix(pieces, mech_real, mech_imag, adjoint):
    real_part, imag_part = pieces
    plain_rr = jnp.einsum("mn,nok->mok", mech_real, real_part, precision=highest)
    plain_ii = jnp.einsum("mn,nok->mok", mech_imag, imag_part, precision=highest)
    plain_ri = jnp.einsum("mn,nok->mok", mech_real, imag_part, precision=highest)
    plain_ir = jnp.einsum("mn,nok->mok", mech_imag, real_part, precision=highest)
    if adjoint:
        return (plain_rr + plain_ii, plain_ri - plain_ir)
    return (plain_rr - plain_ii, plain_ri + plain_ir)


def ket_side(parts, mech_real, mech_imag):
    real_part, imag_part = parts
    local_rows, cav_count, local_cols, width = real_part.shape
    groups = lax.axis_size("row")
    flat = cav_count * local_cols * width
    shaped = (
        real_part.reshape(local_rows, groups, flat // groups),
        imag_part.reshape(local_rows, groups, flat // groups),
    )
    mixed = mech_mix(
        (
            lax.all_to_all(shaped[0], "row", split_axis=1, concat_axis=0, tiled=True),
            lax.all_to_all(shaped[1], "row", split_axis=1, concat_axis=0, tiled=True),
        ),
        mech_real,
        mech_imag,
        False,
    )
    return (
        lax.all_to_all(mixed[0], "row", split_axis=0, concat_axis=1, tiled=True).reshape(
            local_rows, cav_count, local_cols, width
        ),
        lax.all_to_all(mixed[1], "row", split_axis=0, concat_axis=1, tiled=True).reshape(
            local_rows, cav_count, local_cols, width
        ),
    )


def bra_side(parts, mech_real, mech_imag):
    real_part, imag_part = parts
    local_rows, cav_count, local_cols, width = real_part.shape
    groups = lax.axis_size("col")
    flat = local_rows * cav_count * width
    moved_real = jnp.transpose(real_part, (2, 0, 1, 3)).reshape(local_cols, groups, flat // groups)
    moved_imag = jnp.transpose(imag_part, (2, 0, 1, 3)).reshape(local_cols, groups, flat // groups)
    mixed = mech_mix(
        (
            lax.all_to_all(moved_real, "col", split_axis=1, concat_axis=0, tiled=True),
            lax.all_to_all(moved_imag, "col", split_axis=1, concat_axis=0, tiled=True),
        ),
        mech_real,
        mech_imag,
        True,
    )
    back_real = jnp.transpose(
        lax.all_to_all(mixed[0], "col", split_axis=0, concat_axis=1, tiled=True).reshape(
            local_cols, local_rows, cav_count, width
        ),
        (1, 2, 0, 3),
    )
    back_imag = jnp.transpose(
        lax.all_to_all(mixed[1], "col", split_axis=0, concat_axis=1, tiled=True).reshape(
            local_cols, local_rows, cav_count, width
        ),
        (1, 2, 0, 3),
    )
    return (back_real, back_imag)


def general_local(rho_real, rho_imag, cav_real, cav_imag, mech_real, mech_imag):
    block_shape = rho_real.shape
    cav_count = cav_real.shape[0]
    local_rows = mech_real.shape[0] // lax.axis_size("row")
    local_cols = mech_real.shape[0] // lax.axis_size("col")
    shape_four = (local_rows, cav_count, local_cols, cav_count)
    state = (rho_real.reshape(shape_four), rho_imag.reshape(shape_four))
    state = cavity_sides(state, cav_real, cav_imag)
    state = bra_side(ket_side(state, mech_real, mech_imag), mech_real, mech_imag)
    return (state[0].reshape(block_shape), state[1].reshape(block_shape))


LANES = 128
SUB = 8


def set_pieces(groups, size):
    uppers, diagonals = pair_tables(groups)
    table = []
    for i, j in uppers:
        rows = [[(size * k, size * i + k, size * j)] for k in range(size)]
        table.append((rows, rows))
    for i, j in diagonals:
        first, second = [], []
        for k in range(size):
            low, high = (size * k, size * j + k, size * j), (size * i + k, size * i)
            first.append(([low] if k else []) + [(size * k + k,) + (high[0], high[1] + k)])
            upper = [(size * k + k + 1, high[0], high[1] + k + 1)] if k + 1 < size else []
            second.append([low] + upper)
        table.append((first, second))
    return table


def split_high(value):
    high = value.astype(jnp.bfloat16)
    return high, (value - high.astype(jnp.float32)).astype(jnp.bfloat16)


def split_weights(value):
    high = lax.reduce_precision(value, exponent_bits=8, mantissa_bits=7)
    return high.astype(jnp.bfloat16), (value - high).astype(jnp.bfloat16)


def dot3(left, right):
    total = jnp.dot(left[0], right[1], preferred_element_type=jnp.float32)
    total += jnp.dot(left[1], right[0], preferred_element_type=jnp.float32)
    return total + jnp.dot(left[0], right[0], preferred_element_type=jnp.float32)


def row_span(cols):
    return SUB * (cols + 1 - cols % 2)


def lane_index():
    return lax.broadcasted_iota(jnp.int32, (SUB, LANES), 1)


def turn(value, shift):
    return pltpu.roll(value, shift % LANES, 1) if shift % LANES else value


def enter_kernel(dims, *refs):
    cav, cols, period, pad, chunks = dims
    x_refs, (lh, ll, rh, rl) = refs[:2], refs[2:6]
    outs = refs[6 : 6 + chunks]
    work, plain, turned = refs[6 + chunks :]
    lane = lane_index()
    stride = x_refs[0].shape[0] // SUB
    step_rows = period * cols * cav // LANES
    count = cols * SUB
    span = row_span(cols)

    @pl.when(pl.program_id(0) == 0)
    def _():
        work[...] = jnp.zeros_like(work)

    def unroll(outer, carry):
        for part in range(2):
            for inner in range(period):
                for col in range(cols):
                    place = (inner * cols + col) * cav
                    row, shift = outer * step_rows + place // LANES, place % LANES
                    value = x_refs[part][pl.ds(row, SUB, stride=stride), :]
                    if shift + cav > LANES:
                        after = x_refs[part][pl.ds(row + 1, SUB, stride=stride), :]
                        value = jnp.where(lane >= shift, value, after)
                    target = col * SUB * pad + outer * period + inner
                    work[part, pl.ds(target, SUB, stride=pad), :] = turn(value, -shift)
        return carry

    lax.fori_loop(0, cav // period, unroll, 0)

    left = (lh[...], ll[...])
    right = (rh[...], rl[...])

    def mix(pair, carry):
        halves = []
        for extra in range(2):
            start = pl.multiple_of((2 * pair + extra) * pad, SUB)
            halves.append(jnp.concatenate([work[0, pl.ds(start, pad), :], work[1, pl.ds(start, pad), :]], axis=0))
        ket = dot3(left, split_high(jnp.concatenate(halves, axis=1)))
        stacked = jnp.concatenate(
            [
                jnp.concatenate([ket[:pad, lo : lo + LANES], ket[LANES : LANES + pad, lo : lo + LANES]], axis=1)
                for lo in (0, LANES)
            ],
            axis=0,
        )
        both = dot3(split_high(stacked), right)
        for extra in range(2):
            for part in range(2):
                block = both[extra * pad : (extra + 1) * pad, part * LANES : (part + 1) * LANES]
                plain[part, pl.ds(2 * pair + extra, pad, stride=span), :] = block
                square = jnp.concatenate([block, jnp.zeros((LANES - pad, LANES), jnp.float32)], axis=0)
                turned[part, pl.ds(2 * pair + extra, pad, stride=span), :] = jnp.transpose(square)[:pad]
        return carry

    lax.fori_loop(0, count // 2, mix, 0)

    size = cav // 4
    table = set_pieces(4, size)
    end = size * size

    def gather(col, carry):
        for chunk in range(chunks):
            base = chunk * LANES
            for index, pair in enumerate(table):
                for side in range(2):
                    source = (plain, turned)[side]
                    pieces = [piece for row in pair[side] for piece in row]
                    for part in range(2):
                        total = None
                        for at, (first, row, lane_from) in enumerate(pieces):
                            last = pieces[at + 1][0] if at + 1 < len(pieces) else end
                            if last <= base or first >= base + LANES:
                                continue
                            start = pl.multiple_of(row * span + col * SUB, SUB)
                            value = turn(source[part, pl.ds(start, SUB), :], first - base - lane_from)
                            total = value if total is None else jnp.where(lane >= first - base, value, total)
                        if end < base + LANES:
                            total = jnp.where(lane < end - base, total, 0.0)
                        outs[chunk][index, side, part, col] = total
        return carry

    lax.fori_loop(0, cols, gather, 0)


def leave_kernel(dims, *refs):
    cav, cols, period, pad, chunks = dims
    ins, outs = refs[:chunks], refs[chunks : chunks + 2]
    plain, turned = refs[chunks + 2 :]
    lane = lane_index()
    count = cols * SUB
    span = row_span(cols)
    size = cav // 4
    groups = 4
    table = set_pieces(groups, size)
    end = size * size

    def scatter(col, carry):
        for side in range(2):
            target = (plain, turned)[side]
            found = [[] for _ in range(cav)]
            for index, pair in enumerate(table):
                pieces = [piece for row in pair[side] for piece in row]
                for at, (first, row, lane_from) in enumerate(pieces):
                    last = pieces[at + 1][0] if at + 1 < len(pieces) else end
                    while first < last:
                        stop = min(last, (first // LANES + 1) * LANES)
                        found[row].append((lane_from, stop - first, index, first))
                        lane_from, first = lane_from + stop - first, stop
            for row in range(cav):
                for part in range(2):
                    total, reach = None, 0
                    for lane_to, length, index, first in sorted(found[row]):
                        if total is None:
                            total = jnp.zeros((SUB, LANES), jnp.float32)
                        elif lane_to > reach:
                            total = jnp.where(lane >= reach, 0.0, total)
                        value = turn(ins[first // LANES][index, side, part, col], lane_to - first % LANES)
                        total = jnp.where(lane >= lane_to, value, total)
                        reach = lane_to + length
                    if total is None:
                        total = jnp.zeros((SUB, LANES), jnp.float32)
                    else:
                        total = jnp.where(lane < reach, total, 0.0)
                    start = pl.multiple_of(row * span + col * SUB, SUB)
                    target[part, pl.ds(start, SUB), :] = total
        return carry

    lax.fori_loop(0, cols, scatter, 0)

    def merge(index, carry):
        for part in range(2):
            block = turned[part, pl.ds(index, pad, stride=span), :]
            square = jnp.concatenate([block, jnp.zeros((LANES - pad, LANES), jnp.float32)], axis=0)
            rows = pl.ds(index, pad, stride=span)
            plain[part, rows, :] = plain[part, rows, :] + jnp.transpose(square)[:pad]
        return carry

    lax.fori_loop(0, count, merge, 0)

    stride = outs[0].shape[0] // SUB
    step_rows = period * cols * cav // LANES

    def store(outer, carry):
        for part in range(2):
            for inner in range(step_rows):
                begin = inner * LANES
                total = None
                for piece in range(begin // cav, (begin + LANES - 1) // cav + 1):
                    row = (outer * period + piece // cols) * span + (piece % cols) * SUB
                    value = turn(plain[part, pl.ds(pl.multiple_of(row, SUB), SUB), :], piece * cav - begin)
                    total = value if total is None else jnp.where(lane >= piece * cav - begin, value, total)
                outs[part][pl.ds(outer * step_rows + inner, SUB, stride=stride), :] = total
        return carry

    lax.fori_loop(0, cav // period, store, 0)


def kernel_dims(cav, cols):
    period = LANES // math.gcd(cols * cav, LANES)
    pad = -(-cav // SUB) * SUB
    chunks = -(-(cav // 4) ** 2 // LANES)
    return cav, cols, period, pad, chunks


def kernels_fit(rows, cols, cav):
    period = LANES // math.gcd(cols * cav, LANES)
    return rows % SUB == 0 and cols % 2 == 0 and cav % 4 == 0 and cav % period == 0 and 4 * SUB <= cav <= LANES


def enter(x_real, x_imag, cav_real, cav_imag, rows, cols):
    cav = cav_real.shape[0]
    dims = kernel_dims(cav, cols)
    _, _, _, pad, chunks = dims
    lines = cav * cols * cav // LANES * SUB
    steps = rows // SUB

    def put(matrix, height, width):
        return jnp.pad(matrix, ((0, height - cav), (0, width - cav)))

    ket = jnp.block(
        [
            [put(cav_real, LANES, pad), put(-cav_imag, LANES, pad)],
            [put(cav_imag, LANES, pad), put(cav_real, LANES, pad)],
        ]
    )
    bra = jnp.block(
        [
            [put(cav_real.T, LANES, LANES), put(-cav_imag.T, LANES, LANES)],
            [put(cav_imag.T, LANES, LANES), put(cav_real.T, LANES, LANES)],
        ]
    )
    weights = split_weights(ket) + split_weights(bra)
    n_sets = 8
    shape = (n_sets, 2, 2, cols, rows, LANES)
    return pl.pallas_call(
        functools.partial(enter_kernel, dims),
        grid=(steps,),
        in_specs=[pl.BlockSpec((lines, LANES), lambda g: (g, 0))] * 2
        + [pl.BlockSpec(w.shape, lambda g: (0, 0)) for w in weights],
        out_specs=[pl.BlockSpec((n_sets, 2, 2, cols, SUB, LANES), lambda g: (0, 0, 0, 0, g, 0))] * chunks,
        out_shape=[jax.ShapeDtypeStruct(shape, jnp.float32)] * chunks,
        scratch_shapes=[
            pltpu.VMEM((2, cols * SUB * pad, LANES), jnp.float32),
            pltpu.VMEM((2, row_span(cols) * pad, LANES), jnp.float32),
            pltpu.VMEM((2, row_span(cols) * pad, LANES), jnp.float32),
        ],
        compiler_params=pltpu.CompilerParams(vmem_limit_bytes=60 * 1024 * 1024),
        name="enter",
    )(x_real, x_imag, *weights)


def leave(sets, cav, rows, cols):
    dims = kernel_dims(cav, cols)
    _, _, _, pad, chunks = dims
    lines = cav * cols * cav // LANES * SUB
    steps = rows // SUB
    n_sets = 8
    return pl.pallas_call(
        functools.partial(leave_kernel, dims),
        grid=(steps,),
        in_specs=[pl.BlockSpec((n_sets, 2, 2, cols, SUB, LANES), lambda g: (0, 0, 0, 0, g, 0))] * chunks,
        out_specs=[pl.BlockSpec((lines, LANES), lambda g: (g, 0))] * 2,
        out_shape=[jax.ShapeDtypeStruct((lines * steps, LANES), jnp.float32)] * 2,
        scratch_shapes=[
            pltpu.VMEM((2, row_span(cols) * pad, LANES), jnp.float32),
            pltpu.VMEM((2, row_span(cols) * pad, LANES), jnp.float32),
        ],
        compiler_params=pltpu.CompilerParams(vmem_limit_bytes=60 * 1024 * 1024),
        name="leave",
    )(*sets)


def pair_tables(groups):
    uppers = [(i, j) for i in range(groups) for j in range(i + 1, groups)]
    diagonals = [(2 * i, 2 * i + 1) for i in range(groups // 2)]
    return uppers, diagonals


def ket_kernel(base, flags, own_ref, wh_ref, wl_ref, row_ref, end_ref, ends_ref, mids_ref, corner_ref, sent_ref, half_ref):
    halves, cols, rows = base
    width = halves * cols
    own = own_ref[0, :] > 0

    @pl.when(flags[1] == 0)
    def _():
        far = flags[0]

        def own_row(block):
            spot = lax.select(far == 1, 3 - block, block)

            def by_bra(side, part, n):
                return row_ref[spot * halves + n // cols, side, part, n % cols]

            def by_ket(side, part, m):
                pieces = [
                    row_ref.at[spot * halves + h, side, part].reshape(cols * rows, LANES)[pl.ds(m, cols, stride=rows), :]
                    for h in range(halves)
                ]
                return jnp.concatenate(pieces, axis=0)

            return by_bra, by_ket

        def got(ref, start):
            def by_bra(side, part, n):
                return ref[start + n // cols, side, part, n % cols]

            def by_ket(side, part, m):
                pieces = [
                    ref.at[start + h, side, part].reshape(cols * rows, LANES)[pl.ds(m, cols, stride=rows), :]
                    for h in range(halves)
                ]
                return jnp.concatenate(pieces, axis=0)

            return by_bra, by_ket

        here, there = far * halves, (1 - far) * halves
        known = {
            (1, 0): own_row(0),
            (1, 1): own_row(1),
            (1, 2): own_row(2),
            (1, 3): own_row(3),
            (0, 0): got(end_ref, 0),
            (0, 2): got(ends_ref, here),
            (0, 3): got(ends_ref, there),
            (2, 3): got(mids_ref, there),
            (2, 2): got(mids_ref, here),
            (3, 3): got(corner_ref, 0),
        }
        weights = (wh_ref[...], wl_ref[...])

        for block in range(4):

            def step(n, carry, block=block):
                columns = []
                for side in range(2):
                    pieces = []
                    for part in range(2):
                        for p in range(4):
                            if (p, block) in known:
                                pieces.append(known[p, block][0](side, part, n))
                            else:
                                read = known[block, p][1]
                                value = jnp.where(own, read(side, part, n), read(1 - side, part, n))
                                pieces.append(-value if part else value)
                    columns.append(jnp.concatenate(pieces, axis=0))
                result = dot3(weights, split_high(jnp.concatenate(columns, axis=1)))
                for side in range(2):
                    lanes = slice(side * LANES, (side + 1) * LANES)
                    for part in range(2):
                        top = part * 2 * rows
                        if block:
                            sent_ref[side, part, (block - 1) * width + n] = result[top : top + rows, lanes]
                        half_ref[side, part, block * width + n] = result[top + rows : top + 2 * rows, lanes]
                return carry

            lax.fori_loop(0, width, step, 0)


def bra_kernel(base, flags, own_ref, eh_ref, el_ref, bh_ref, bl_ref, row_ref, part_ref, half_ref, out_ref, work):
    halves, cols, rows = base
    width = halves * cols
    mech = 4 * width
    span = row_span(rows // SUB)
    own = own_ref[0, :] > 0
    far = flags[0]

    def spot_of(block):
        return lax.select(far == 1, 3 - block, block)

    @pl.when(flags[1] == 1)
    def _():
        def by_ket(block, side, part, m):
            pieces = [
                row_ref.at[spot_of(block) * halves + h, side, part].reshape(cols * rows, LANES)[
                    pl.ds(m, cols, stride=rows), :
                ]
                for h in range(halves)
            ]
            return jnp.concatenate(pieces, axis=0)

        weights = (eh_ref[...], el_ref[...])

        for block in range(4):

            def step(n, carry, block=block):
                columns = []
                for side in range(2):
                    pieces = []
                    for part in range(2):
                        pieces.append(row_ref[spot_of(block) * halves + n // cols, side, part, n % cols])
                        for p in range(1, 4):
                            if block:
                                pieces.append(jnp.zeros((rows, LANES), jnp.float32))
                            else:
                                value = jnp.where(own, by_ket(p, side, part, n), by_ket(p, 1 - side, part, n))
                                pieces.append(-value if part else value)
                    columns.append(jnp.concatenate(pieces, axis=0))
                result = dot3(weights, split_high(jnp.concatenate(columns, axis=1)))
                for side in range(2):
                    for part in range(2):
                        value = result[part * rows : (part + 1) * rows, side * LANES : (side + 1) * LANES]
                        if block:
                            value = value + part_ref[side, part, (block - 1) * width + n]
                        work[side, part, pl.ds(pl.multiple_of((block * width + n) * span, SUB), rows), :] = value
                return carry

            lax.fori_loop(0, width, step, 0)

    @pl.when(flags[1] == 0)
    def _():
        def step(n, carry):
            for side in range(2):
                for part in range(2):
                    work[side, part, pl.ds(pl.multiple_of(n * span, SUB), rows), :] = half_ref[side, part, n]
            return carry

        lax.fori_loop(0, mech, step, 0)

    weights = (bh_ref[...], bl_ref[...])

    def finish(m, carry):
        columns = [
            jnp.concatenate([work[side, part, pl.ds(m, mech, stride=span), :] for part in range(2)], axis=0)
            for side in range(2)
        ]
        result = dot3(weights, split_high(jnp.concatenate(columns, axis=1)))
        for side in range(2):
            for part in range(2):
                value = result[part * mech : (part + 1) * mech, side * LANES : (side + 1) * LANES]
                work[side, part, pl.ds(m, mech, stride=span), :] = value
        return carry

    lax.fori_loop(0, rows, finish, 0)

    def put(q, carry):
        spot = lax.select(far == 1, 3 - q // width, q // width)
        for side in range(2):
            for part in range(2):
                value = work[side, part, pl.ds(pl.multiple_of(q * span, SUB), rows), :]
                out_ref[spot * halves + q % width // cols, side, part, q % cols] = value
        return carry

    lax.fori_loop(0, mech, put, 0)


def whole_block(shape):
    return pl.BlockSpec(shape, lambda g, flags: (0,) * len(shape))


LIMIT = 48 * 1024 * 1024


def pick_blocks(got, flags):
    halves = got.shape[0] // 4
    far = flags[0] == 1

    def blocks(near, away, count):
        return lax.dynamic_slice_in_dim(got, jnp.where(far, away, near) * halves, count * halves, 0)

    return blocks(0, 3, 1), blocks(2, 0, 2), blocks(0, 2, 2)


INNER = [(0, 1), (3, 2)]
CROSS = [(1, 2), (2, 1)]
BACK = [(1, 0), (2, 3)]


def mix_kets(got, end, ends, mids, corner, own, flags, weights):
    members, _, _, cols, rows, _ = got.shape
    halves = members // 4
    width = halves * cols
    args = (own, weights[0], weights[1], got, end, ends, mids, corner)
    shapes = ((2, 2, 3 * width, rows, LANES), (2, 2, 4 * width, rows, LANES))
    sent, half = pl.pallas_call(
        functools.partial(ket_kernel, (halves, cols, rows)),
        grid_spec=pltpu.PrefetchScalarGridSpec(
            num_scalar_prefetch=1,
            grid=(1,),
            in_specs=[whole_block(a.shape) for a in args],
            out_specs=[whole_block(shape) for shape in shapes],
        ),
        out_shape=[jax.ShapeDtypeStruct(shape, jnp.float32) for shape in shapes],
        compiler_params=pltpu.CompilerParams(vmem_limit_bytes=LIMIT),
        cost_estimate=pl.CostEstimate(flops=12_000_000_000, bytes_accessed=40_000_000, transcendentals=0),
        name="ket",
    )(flags, *args)
    return sent, half


def mix_bras(got, partial, half, own, flags, end_line, bra):
    members, _, _, cols, rows, _ = got.shape
    halves = members // 4
    args = (own, end_line[0], end_line[1], bra[0], bra[1], got, partial, half)
    return pl.pallas_call(
        functools.partial(bra_kernel, (halves, cols, rows)),
        grid_spec=pltpu.PrefetchScalarGridSpec(
            num_scalar_prefetch=1,
            grid=(1,),
            in_specs=[whole_block(a.shape) for a in args],
            out_specs=whole_block(got.shape),
            scratch_shapes=[pltpu.VMEM((2, 2, members * cols * row_span(rows // SUB), LANES), jnp.float32)],
        ),
        out_shape=jax.ShapeDtypeStruct(got.shape, jnp.float32),
        compiler_params=pltpu.CompilerParams(vmem_limit_bytes=LIMIT),
        cost_estimate=pl.CostEstimate(flops=12_000_000_000, bytes_accessed=40_000_000, transcendentals=0),
        name="bra",
    )(flags, *args)


def swap_plane(array):
    return lax.all_to_all(array, "col", split_axis=0, concat_axis=0, tiled=True)


def realified(real_part, imag_part, sign):
    top = jnp.concatenate([real_part, -sign * imag_part], axis=1)
    bottom = jnp.concatenate([sign * imag_part, real_part], axis=1)
    return split_weights(jnp.concatenate([top, bottom], axis=0))


def fast_local(rho_real, rho_imag, cav_real, cav_imag, mech_real, mech_imag):
    block_shape = rho_real.shape
    cav = cav_real.shape[0]
    mech = mech_real.shape[0]
    n_row, n_col = lax.axis_size("row"), lax.axis_size("col")
    rows, cols = mech // n_row, mech // n_col
    size = cav // n_row
    sets = enter(
        rho_real.reshape(-1, LANES), rho_imag.reshape(-1, LANES), cav_real, cav_imag, rows, cols
    )
    chunks = len(sets)

    place = lax.axis_index("row")
    member = lax.axis_index("col")
    far_half = place >= n_row // 2
    is_end = (place == 0) | (place == n_row - 1)
    flags = jnp.stack([far_half, is_end]).astype(jnp.int32)
    lanes = jnp.arange(chunks * LANES)
    uppers, _ = pair_tables(n_row)
    own_lanes = ((member >= len(uppers)) & ((lanes // size) == (lanes % size))).astype(jnp.int32)

    def order(matrix):
        shaped = matrix.reshape(n_row, rows, n_row, rows)
        return jnp.where(far_half, shaped[::-1, :, ::-1], shaped).reshape(mech, mech)

    mixer_real, mixer_imag = order(mech_real), order(mech_imag)
    outside = (jnp.arange(mech) >= rows)[None, :]
    away_real = jnp.where(outside, mixer_real[:rows], 0.0)
    away_imag = jnp.where(outside, mixer_imag[:rows], 0.0)
    whole = realified(
        jnp.concatenate([away_real, mixer_real[rows : 2 * rows]]),
        jnp.concatenate([away_imag, mixer_imag[rows : 2 * rows]]),
        1.0,
    )
    end_line = realified(mixer_real[:rows], mixer_imag[:rows], 1.0)
    bra = realified(mixer_real, mixer_imag, -1.0)
    own = [own_lanes[chunk * LANES : (chunk + 1) * LANES][None] for chunk in range(chunks)]

    state = {("set", chunk): sets[chunk] for chunk in range(chunks)}
    for tick in range(chunks + 5):
        fresh, moved, mixed, sent, last, gone = (tick - back for back in range(6))
        made = {}
        if fresh < chunks:
            made["row", fresh] = swap_plane(state.pop(("set", fresh)))
        if 0 <= gone < chunks:
            made["done", gone] = swap_plane(state.pop(("out", gone)))
        if 0 <= moved < chunks:
            end, ends, mids = pick_blocks(state["row", moved], flags)
            made["end", moved] = lax.ppermute(end, "row", INNER)
            made["ends", moved] = lax.ppermute(ends, "row", INNER)
            made["mids", moved] = lax.ppermute(mids, "row", CROSS)
        if 0 <= sent < chunks:
            made["partial", sent] = lax.ppermute(state.pop(("sent", sent)), "row", BACK)
        if 0 <= mixed < chunks:
            end, ends, mids = (state.pop((name, mixed)) for name in ("end", "ends", "mids"))
            corner = lax.ppermute(end, "row", CROSS)
            made["sent", mixed], made["mine", mixed] = mix_kets(
                state["row", mixed], end, ends, mids, corner, own[mixed], flags, whole
            )
        if 0 <= last < chunks:
            parts = [state.pop((name, last)) for name in ("row", "partial", "mine")]
            made["out", last] = mix_bras(*parts, own[last], flags, end_line, bra)
        state.update(made)
        names = sorted(state)
        state.update(zip(names, lax.optimization_barrier([state[name] for name in names])))
    results = [state["done", chunk] for chunk in range(chunks)]
    final = leave(results, cav, rows, cols)
    return final[0].reshape(block_shape), final[1].reshape(block_shape)


def fits(mesh, mech, cav):
    n_row, n_col = mesh.shape["row"], mesh.shape["col"]
    if n_row != 4 or n_col != 2 * n_row or mech % n_col:
        return False
    return kernels_fit(mech // n_row, mech // n_col, cav)


def solution(mesh):
    def whole(rho_real, rho_imag, cav_real, cav_imag, mech_real, mech_imag):
        local = fast_local if fits(mesh, mech_real.shape[0], cav_real.shape[0]) else general_local
        return jax.shard_map(
            local,
            mesh=mesh,
            in_specs=(P("row", "col", None), P("row", "col", None), P(), P(), P(), P()),
            out_specs=(P("row", "col", None), P("row", "col", None)),
            check_vma=False,
        )(rho_real, rho_imag, cav_real, cav_imag, mech_real, mech_imag)

    return whole
```

```python
import functools
import math

import jax
import jax.numpy as jnp
from jax import lax
from jax.experimental import pallas as pl
from jax.experimental.pallas import tpu as pltpu
from jax.sharding import PartitionSpec as P

highest = lax.Precision.HIGHEST


def cavity_sides(parts, cav_real, cav_imag):
    real_part, imag_part = parts
    left_real = jnp.einsum("cd,mdne->mcne", cav_real, real_part, precision=highest) - jnp.einsum(
        "cd,mdne->mcne", cav_imag, imag_part, precision=highest
    )
    left_imag = jnp.einsum("cd,mdne->mcne", cav_real, imag_part, precision=highest) + jnp.einsum(
        "cd,mdne->mcne", cav_imag, real_part, precision=highest
    )
    right_real = jnp.einsum("mcne,fe->mcnf", left_real, cav_real, precision=highest) + jnp.einsum(
        "mcne,fe->mcnf", left_imag, cav_imag, precision=highest
    )
    right_imag = jnp.einsum("mcne,fe->mcnf", left_imag, cav_real, precision=highest) - jnp.einsum(
        "mcne,fe->mcnf", left_real, cav_imag, precision=highest
    )
    return (right_real, right_imag)


def mech_mix(pieces, mech_real, mech_imag, adjoint):
    real_part, imag_part = pieces
    plain_rr = jnp.einsum("mn,nok->mok", mech_real, real_part, precision=highest)
    plain_ii = jnp.einsum("mn,nok->mok", mech_imag, imag_part, precision=highest)
    plain_ri = jnp.einsum("mn,nok->mok", mech_real, imag_part, precision=highest)
    plain_ir = jnp.einsum("mn,nok->mok", mech_imag, real_part, precision=highest)
    if adjoint:
        return (plain_rr + plain_ii, plain_ri - plain_ir)
    return (plain_rr - plain_ii, plain_ri + plain_ir)


def ket_side(parts, mech_real, mech_imag):
    real_part, imag_part = parts
    local_rows, cav_count, local_cols, width = real_part.shape
    groups = lax.axis_size("row")
    flat = cav_count * local_cols * width
    shaped = (
        real_part.reshape(local_rows, groups, flat // groups),
        imag_part.reshape(local_rows, groups, flat // groups),
    )
    mixed = mech_mix(
        (
            lax.all_to_all(shaped[0], "row", split_axis=1, concat_axis=0, tiled=True),
            lax.all_to_all(shaped[1], "row", split_axis=1, concat_axis=0, tiled=True),
        ),
        mech_real,
        mech_imag,
        False,
    )
    return (
        lax.all_to_all(mixed[0], "row", split_axis=0, concat_axis=1, tiled=True).reshape(
            local_rows, cav_count, local_cols, width
        ),
        lax.all_to_all(mixed[1], "row", split_axis=0, concat_axis=1, tiled=True).reshape(
            local_rows, cav_count, local_cols, width
        ),
    )


def bra_side(parts, mech_real, mech_imag):
    real_part, imag_part = parts
    local_rows, cav_count, local_cols, width = real_part.shape
    groups = lax.axis_size("col")
    flat = local_rows * cav_count * width
    moved_real = jnp.transpose(real_part, (2, 0, 1, 3)).reshape(local_cols, groups, flat // groups)
    moved_imag = jnp.transpose(imag_part, (2, 0, 1, 3)).reshape(local_cols, groups, flat // groups)
    mixed = mech_mix(
        (
            lax.all_to_all(moved_real, "col", split_axis=1, concat_axis=0, tiled=True),
            lax.all_to_all(moved_imag, "col", split_axis=1, concat_axis=0, tiled=True),
        ),
        mech_real,
        mech_imag,
        True,
    )
    back_real = jnp.transpose(
        lax.all_to_all(mixed[0], "col", split_axis=0, concat_axis=1, tiled=True).reshape(
            local_cols, local_rows, cav_count, width
        ),
        (1, 2, 0, 3),
    )
    back_imag = jnp.transpose(
        lax.all_to_all(mixed[1], "col", split_axis=0, concat_axis=1, tiled=True).reshape(
            local_cols, local_rows, cav_count, width
        ),
        (1, 2, 0, 3),
    )
    return (back_real, back_imag)


def general_local(rho_real, rho_imag, cav_real, cav_imag, mech_real, mech_imag):
    block_shape = rho_real.shape
    cav_count = cav_real.shape[0]
    local_rows = mech_real.shape[0] // lax.axis_size("row")
    local_cols = mech_real.shape[0] // lax.axis_size("col")
    shape_four = (local_rows, cav_count, local_cols, cav_count)
    state = (rho_real.reshape(shape_four), rho_imag.reshape(shape_four))
    state = cavity_sides(state, cav_real, cav_imag)
    state = bra_side(ket_side(state, mech_real, mech_imag), mech_real, mech_imag)
    return (state[0].reshape(block_shape), state[1].reshape(block_shape))


LANES = 128
SUB = 8


def set_pieces(groups, size):
    uppers, diagonals = pair_tables(groups)
    table = []
    for i, j in uppers:
        rows = [[(size * k, size * i + k, size * j)] for k in range(size)]
        table.append((rows, rows))
    for i, j in diagonals:
        first, second = [], []
        for k in range(size):
            low, high = (size * k, size * j + k, size * j), (size * i + k, size * i)
            first.append(([low] if k else []) + [(size * k + k,) + (high[0], high[1] + k)])
            upper = [(size * k + k + 1, high[0], high[1] + k + 1)] if k + 1 < size else []
            second.append([low] + upper)
        table.append((first, second))
    return table


def split_high(value):
    high = value.astype(jnp.bfloat16)
    return high, (value - high.astype(jnp.float32)).astype(jnp.bfloat16)


def split_weights(value):
    high = lax.reduce_precision(value, exponent_bits=8, mantissa_bits=7)
    return high.astype(jnp.bfloat16), (value - high).astype(jnp.bfloat16)


def dot3(left, right):
    total = jnp.dot(left[0], right[1], preferred_element_type=jnp.float32)
    total += jnp.dot(left[1], right[0], preferred_element_type=jnp.float32)
    return total + jnp.dot(left[0], right[0], preferred_element_type=jnp.float32)


def row_span(cols):
    return SUB * (cols + 1 - cols % 2)


def lane_index():
    return lax.broadcasted_iota(jnp.int32, (SUB, LANES), 1)


def turn(value, shift):
    return pltpu.roll(value, shift % LANES, 1) if shift % LANES else value


def enter_kernel(dims, *refs):
    cav, cols, period, pad, chunks = dims
    x_refs, (lh, ll, rh, rl) = refs[:2], refs[2:6]
    outs = refs[6 : 6 + chunks]
    work, plain, turned = refs[6 + chunks :]
    lane = lane_index()
    stride = x_refs[0].shape[0] // SUB
    step_rows = period * cols * cav // LANES
    count = cols * SUB
    span = row_span(cols)

    @pl.when(pl.program_id(0) == 0)
    def _():
        work[...] = jnp.zeros_like(work)

    def unroll(outer, carry):
        for part in range(2):
            for inner in range(period):
                for col in range(cols):
                    place = (inner * cols + col) * cav
                    row, shift = outer * step_rows + place // LANES, place % LANES
                    value = x_refs[part][pl.ds(row, SUB, stride=stride), :]
                    if shift + cav > LANES:
                        after = x_refs[part][pl.ds(row + 1, SUB, stride=stride), :]
                        value = jnp.where(lane >= shift, value, after)
                    target = col * SUB * pad + outer * period + inner
                    work[part, pl.ds(target, SUB, stride=pad), :] = turn(value, -shift)
        return carry

    lax.fori_loop(0, cav // period, unroll, 0)

    left = (lh[...], ll[...])
    right = (rh[...], rl[...])

    def mix(pair, carry):
        halves = []
        for extra in range(2):
            start = pl.multiple_of((2 * pair + extra) * pad, SUB)
            halves.append(jnp.concatenate([work[0, pl.ds(start, pad), :], work[1, pl.ds(start, pad), :]], axis=0))
        ket = dot3(left, split_high(jnp.concatenate(halves, axis=1)))
        stacked = jnp.concatenate(
            [
                jnp.concatenate([ket[:pad, lo : lo + LANES], ket[LANES : LANES + pad, lo : lo + LANES]], axis=1)
                for lo in (0, LANES)
            ],
            axis=0,
        )
        both = dot3(split_high(stacked), right)
        for extra in range(2):
            for part in range(2):
                block = both[extra * pad : (extra + 1) * pad, part * LANES : (part + 1) * LANES]
                plain[part, pl.ds(2 * pair + extra, pad, stride=span), :] = block
                square = jnp.concatenate([block, jnp.zeros((LANES - pad, LANES), jnp.float32)], axis=0)
                turned[part, pl.ds(2 * pair + extra, pad, stride=span), :] = jnp.transpose(square)[:pad]
        return carry

    lax.fori_loop(0, count // 2, mix, 0)

    size = cav // 4
    table = set_pieces(4, size)
    end = size * size

    def gather(col, carry):
        for chunk in range(chunks):
            base = chunk * LANES
            for index, pair in enumerate(table):
                for side in range(2):
                    source = (plain, turned)[side]
                    pieces = [piece for row in pair[side] for piece in row]
                    for part in range(2):
                        total = None
                        for at, (first, row, lane_from) in enumerate(pieces):
                            last = pieces[at + 1][0] if at + 1 < len(pieces) else end
                            if last <= base or first >= base + LANES:
                                continue
                            start = pl.multiple_of(row * span + col * SUB, SUB)
                            value = turn(source[part, pl.ds(start, SUB), :], first - base - lane_from)
                            total = value if total is None else jnp.where(lane >= first - base, value, total)
                        if end < base + LANES:
                            total = jnp.where(lane < end - base, total, 0.0)
                        outs[chunk][index, side, part, col] = total
        return carry

    lax.fori_loop(0, cols, gather, 0)


def leave_kernel(dims, *refs):
    cav, cols, period, pad, chunks = dims
    ins, outs = refs[:chunks], refs[chunks : chunks + 2]
    plain, turned = refs[chunks + 2 :]
    lane = lane_index()
    count = cols * SUB
    span = row_span(cols)
    size = cav // 4
    groups = 4
    table = set_pieces(groups, size)
    end = size * size

    def scatter(col, carry):
        for side in range(2):
            target = (plain, turned)[side]
            found = [[] for _ in range(cav)]
            for index, pair in enumerate(table):
                pieces = [piece for row in pair[side] for piece in row]
                for at, (first, row, lane_from) in enumerate(pieces):
                    last = pieces[at + 1][0] if at + 1 < len(pieces) else end
                    while first < last:
                        stop = min(last, (first // LANES + 1) * LANES)
                        found[row].append((lane_from, stop - first, index, first))
                        lane_from, first = lane_from + stop - first, stop
            for row in range(cav):
                for part in range(2):
                    total, reach = None, 0
                    for lane_to, length, index, first in sorted(found[row]):
                        if total is None:
                            total = jnp.zeros((SUB, LANES), jnp.float32)
                        elif lane_to > reach:
                            total = jnp.where(lane >= reach, 0.0, total)
                        value = turn(ins[first // LANES][index, side, part, col], lane_to - first % LANES)
                        total = jnp.where(lane >= lane_to, value, total)
                        reach = lane_to + length
                    if total is None:
                        total = jnp.zeros((SUB, LANES), jnp.float32)
                    else:
                        total = jnp.where(lane < reach, total, 0.0)
                    start = pl.multiple_of(row * span + col * SUB, SUB)
                    target[part, pl.ds(start, SUB), :] = total
        return carry

    lax.fori_loop(0, cols, scatter, 0)

    def merge(index, carry):
        for part in range(2):
            block = turned[part, pl.ds(index, pad, stride=span), :]
            square = jnp.concatenate([block, jnp.zeros((LANES - pad, LANES), jnp.float32)], axis=0)
            rows = pl.ds(index, pad, stride=span)
            plain[part, rows, :] = plain[part, rows, :] + jnp.transpose(square)[:pad]
        return carry

    lax.fori_loop(0, count, merge, 0)

    stride = outs[0].shape[0] // SUB
    step_rows = period * cols * cav // LANES

    def store(outer, carry):
        for part in range(2):
            for inner in range(step_rows):
                begin = inner * LANES
                total = None
                for piece in range(begin // cav, (begin + LANES - 1) // cav + 1):
                    row = (outer * period + piece // cols) * span + (piece % cols) * SUB
                    value = turn(plain[part, pl.ds(pl.multiple_of(row, SUB), SUB), :], piece * cav - begin)
                    total = value if total is None else jnp.where(lane >= piece * cav - begin, value, total)
                outs[part][pl.ds(outer * step_rows + inner, SUB, stride=stride), :] = total
        return carry

    lax.fori_loop(0, cav // period, store, 0)


def kernel_dims(cav, cols):
    period = LANES // math.gcd(cols * cav, LANES)
    pad = -(-cav // SUB) * SUB
    chunks = -(-(cav // 4) ** 2 // LANES)
    return cav, cols, period, pad, chunks


def kernels_fit(rows, cols, cav):
    period = LANES // math.gcd(cols * cav, LANES)
    return rows % SUB == 0 and cols % 2 == 0 and cav % 4 == 0 and cav % period == 0 and 4 * SUB <= cav <= LANES


def enter(x_real, x_imag, cav_real, cav_imag, rows, cols):
    cav = cav_real.shape[0]
    dims = kernel_dims(cav, cols)
    _, _, _, pad, chunks = dims
    lines = cav * cols * cav // LANES * SUB
    steps = rows // SUB

    def put(matrix, height, width):
        return jnp.pad(matrix, ((0, height - cav), (0, width - cav)))

    ket = jnp.block(
        [
            [put(cav_real, LANES, pad), put(-cav_imag, LANES, pad)],
            [put(cav_imag, LANES, pad), put(cav_real, LANES, pad)],
        ]
    )
    bra = jnp.block(
        [
            [put(cav_real.T, LANES, LANES), put(-cav_imag.T, LANES, LANES)],
            [put(cav_imag.T, LANES, LANES), put(cav_real.T, LANES, LANES)],
        ]
    )
    weights = split_weights(ket) + split_weights(bra)
    n_sets = 8
    shape = (n_sets, 2, 2, cols, rows, LANES)
    return pl.pallas_call(
        functools.partial(enter_kernel, dims),
        grid=(steps,),
        in_specs=[pl.BlockSpec((lines, LANES), lambda g: (g, 0))] * 2
        + [pl.BlockSpec(w.shape, lambda g: (0, 0)) for w in weights],
        out_specs=[pl.BlockSpec((n_sets, 2, 2, cols, SUB, LANES), lambda g: (0, 0, 0, 0, g, 0))] * chunks,
        out_shape=[jax.ShapeDtypeStruct(shape, jnp.float32)] * chunks,
        scratch_shapes=[
            pltpu.VMEM((2, cols * SUB * pad, LANES), jnp.float32),
            pltpu.VMEM((2, row_span(cols) * pad, LANES), jnp.float32),
            pltpu.VMEM((2, row_span(cols) * pad, LANES), jnp.float32),
        ],
        compiler_params=pltpu.CompilerParams(vmem_limit_bytes=60 * 1024 * 1024),
        name="enter",
    )(x_real, x_imag, *weights)


def leave(sets, cav, rows, cols):
    dims = kernel_dims(cav, cols)
    _, _, _, pad, chunks = dims
    lines = cav * cols * cav // LANES * SUB
    steps = rows // SUB
    n_sets = 8
    return pl.pallas_call(
        functools.partial(leave_kernel, dims),
        grid=(steps,),
        in_specs=[pl.BlockSpec((n_sets, 2, 2, cols, SUB, LANES), lambda g: (0, 0, 0, 0, g, 0))] * chunks,
        out_specs=[pl.BlockSpec((lines, LANES), lambda g: (g, 0))] * 2,
        out_shape=[jax.ShapeDtypeStruct((lines * steps, LANES), jnp.float32)] * 2,
        scratch_shapes=[
            pltpu.VMEM((2, row_span(cols) * pad, LANES), jnp.float32),
            pltpu.VMEM((2, row_span(cols) * pad, LANES), jnp.float32),
        ],
        compiler_params=pltpu.CompilerParams(vmem_limit_bytes=60 * 1024 * 1024),
        name="leave",
    )(*sets)


def pair_tables(groups):
    uppers = [(i, j) for i in range(groups) for j in range(i + 1, groups)]
    diagonals = [(2 * i, 2 * i + 1) for i in range(groups // 2)]
    return uppers, diagonals


def ket_kernel(base, flags, own_ref, wh_ref, wl_ref, row_ref, end_ref, ends_ref, mids_ref, corner_ref, sent_ref, half_ref):
    halves, cols, rows = base
    width = halves * cols
    own = own_ref[0, :] > 0

    @pl.when(flags[1] == 0)
    def _():
        far = flags[0]

        def own_row(block):
            spot = lax.select(far == 1, 3 - block, block)

            def by_bra(side, part, n):
                return row_ref[spot * halves + n // cols, side, part, n % cols]

            def by_ket(side, part, m):
                pieces = [
                    row_ref.at[spot * halves + h, side, part].reshape(cols * rows, LANES)[pl.ds(m, cols, stride=rows), :]
                    for h in range(halves)
                ]
                return jnp.concatenate(pieces, axis=0)

            return by_bra, by_ket

        def got(ref, start):
            def by_bra(side, part, n):
                return ref[start + n // cols, side, part, n % cols]

            def by_ket(side, part, m):
                pieces = [
                    ref.at[start + h, side, part].reshape(cols * rows, LANES)[pl.ds(m, cols, stride=rows), :]
                    for h in range(halves)
                ]
                return jnp.concatenate(pieces, axis=0)

            return by_bra, by_ket

        here, there = far * halves, (1 - far) * halves
        known = {
            (1, 0): own_row(0),
            (1, 1): own_row(1),
            (1, 2): own_row(2),
            (1, 3): own_row(3),
            (0, 0): got(end_ref, 0),
            (0, 2): got(ends_ref, here),
            (0, 3): got(ends_ref, there),
            (2, 3): got(mids_ref, there),
            (2, 2): got(mids_ref, here),
            (3, 3): got(corner_ref, 0),
        }
        weights = (wh_ref[...], wl_ref[...])

        for block in range(4):

            def step(n, carry, block=block):
                columns = []
                for side in range(2):
                    pieces = []
                    for part in range(2):
                        for p in range(4):
                            if (p, block) in known:
                                pieces.append(known[p, block][0](side, part, n))
                            else:
                                read = known[block, p][1]
                                value = jnp.where(own, read(side, part, n), read(1 - side, part, n))
                                pieces.append(-value if part else value)
                    columns.append(jnp.concatenate(pieces, axis=0))
                result = dot3(weights, split_high(jnp.concatenate(columns, axis=1)))
                for side in range(2):
                    lanes = slice(side * LANES, (side + 1) * LANES)
                    for part in range(2):
                        top = part * 2 * rows
                        if block:
                            sent_ref[side, part, (block - 1) * width + n] = result[top : top + rows, lanes]
                        half_ref[side, part, block * width + n] = result[top + rows : top + 2 * rows, lanes]
                return carry

            lax.fori_loop(0, width, step, 0)


def bra_kernel(base, flags, own_ref, eh_ref, el_ref, bh_ref, bl_ref, row_ref, part_ref, half_ref, out_ref, work):
    halves, cols, rows = base
    width = halves * cols
    mech = 4 * width
    span = row_span(rows // SUB)
    own = own_ref[0, :] > 0
    far = flags[0]

    def spot_of(block):
        return lax.select(far == 1, 3 - block, block)

    @pl.when(flags[1] == 1)
    def _():
        def by_ket(block, side, part, m):
            pieces = [
                row_ref.at[spot_of(block) * halves + h, side, part].reshape(cols * rows, LANES)[
                    pl.ds(m, cols, stride=rows), :
                ]
                for h in range(halves)
            ]
            return jnp.concatenate(pieces, axis=0)

        weights = (eh_ref[...], el_ref[...])

        for block in range(4):

            def step(n, carry, block=block):
                columns = []
                for side in range(2):
                    pieces = []
                    for part in range(2):
                        pieces.append(row_ref[spot_of(block) * halves + n // cols, side, part, n % cols])
                        for p in range(1, 4):
                            if block:
                                pieces.append(jnp.zeros((rows, LANES), jnp.float32))
                            else:
                                value = jnp.where(own, by_ket(p, side, part, n), by_ket(p, 1 - side, part, n))
                                pieces.append(-value if part else value)
                    columns.append(jnp.concatenate(pieces, axis=0))
                result = dot3(weights, split_high(jnp.concatenate(columns, axis=1)))
                for side in range(2):
                    for part in range(2):
                        value = result[part * rows : (part + 1) * rows, side * LANES : (side + 1) * LANES]
                        if block:
                            value = value + part_ref[side, part, (block - 1) * width + n]
                        work[side, part, pl.ds(pl.multiple_of((block * width + n) * span, SUB), rows), :] = value
                return carry

            lax.fori_loop(0, width, step, 0)

    @pl.when(flags[1] == 0)
    def _():
        def step(n, carry):
            for side in range(2):
                for part in range(2):
                    work[side, part, pl.ds(pl.multiple_of(n * span, SUB), rows), :] = half_ref[side, part, n]
            return carry

        lax.fori_loop(0, mech, step, 0)

    weights = (bh_ref[...], bl_ref[...])

    def finish(m, carry):
        columns = [
            jnp.concatenate([work[side, part, pl.ds(m, mech, stride=span), :] for part in range(2)], axis=0)
            for side in range(2)
        ]
        result = dot3(weights, split_high(jnp.concatenate(columns, axis=1)))
        for side in range(2):
            for part in range(2):
                value = result[part * mech : (part + 1) * mech, side * LANES : (side + 1) * LANES]
                work[side, part, pl.ds(m, mech, stride=span), :] = value
        return carry

    lax.fori_loop(0, rows, finish, 0)

    def put(q, carry):
        spot = lax.select(far == 1, 3 - q // width, q // width)
        for side in range(2):
            for part in range(2):
                value = work[side, part, pl.ds(pl.multiple_of(q * span, SUB), rows), :]
                out_ref[spot * halves + q % width // cols, side, part, q % cols] = value
        return carry

    lax.fori_loop(0, mech, put, 0)


def whole_block(shape):
    return pl.BlockSpec(shape, lambda g, flags: (0,) * len(shape))


LIMIT = 48 * 1024 * 1024


def pick_blocks(got, flags):
    halves = got.shape[0] // 4
    far = flags[0] == 1

    def blocks(near, away, count):
        return lax.dynamic_slice_in_dim(got, jnp.where(far, away, near) * halves, count * halves, 0)

    return blocks(0, 3, 1), blocks(2, 0, 2), blocks(0, 2, 2)


INNER = [(0, 1), (3, 2)]
CROSS = [(1, 2), (2, 1)]
BACK = [(1, 0), (2, 3)]


def mix_kets(got, end, ends, mids, corner, own, flags, weights):
    members, _, _, cols, rows, _ = got.shape
    halves = members // 4
    width = halves * cols
    args = (own, weights[0], weights[1], got, end, ends, mids, corner)
    shapes = ((2, 2, 3 * width, rows, LANES), (2, 2, 4 * width, rows, LANES))
    sent, half = pl.pallas_call(
        functools.partial(ket_kernel, (halves, cols, rows)),
        grid_spec=pltpu.PrefetchScalarGridSpec(
            num_scalar_prefetch=1,
            grid=(1,),
            in_specs=[whole_block(a.shape) for a in args],
            out_specs=[whole_block(shape) for shape in shapes],
        ),
        out_shape=[jax.ShapeDtypeStruct(shape, jnp.float32) for shape in shapes],
        compiler_params=pltpu.CompilerParams(vmem_limit_bytes=LIMIT),
        cost_estimate=pl.CostEstimate(flops=12_000_000_000, bytes_accessed=40_000_000, transcendentals=0),
        name="ket",
    )(flags, *args)
    return sent, half


def mix_bras(got, partial, half, own, flags, end_line, bra):
    members, _, _, cols, rows, _ = got.shape
    halves = members // 4
    args = (own, end_line[0], end_line[1], bra[0], bra[1], got, partial, half)
    return pl.pallas_call(
        functools.partial(bra_kernel, (halves, cols, rows)),
        grid_spec=pltpu.PrefetchScalarGridSpec(
            num_scalar_prefetch=1,
            grid=(1,),
            in_specs=[whole_block(a.shape) for a in args],
            out_specs=whole_block(got.shape),
            scratch_shapes=[pltpu.VMEM((2, 2, members * cols * row_span(rows // SUB), LANES), jnp.float32)],
        ),
        out_shape=jax.ShapeDtypeStruct(got.shape, jnp.float32),
        compiler_params=pltpu.CompilerParams(vmem_limit_bytes=LIMIT),
        cost_estimate=pl.CostEstimate(flops=12_000_000_000, bytes_accessed=40_000_000, transcendentals=0),
        name="bra",
    )(flags, *args)


def swap_plane(array):
    return lax.all_to_all(array, "col", split_axis=0, concat_axis=0, tiled=True)


def realified(real_part, imag_part, sign):
    top = jnp.concatenate([real_part, -sign * imag_part], axis=1)
    bottom = jnp.concatenate([sign * imag_part, real_part], axis=1)
    return split_weights(jnp.concatenate([top, bottom], axis=0))


def fast_local(rho_real, rho_imag, cav_real, cav_imag, mech_real, mech_imag):
    block_shape = rho_real.shape
    cav = cav_real.shape[0]
    mech = mech_real.shape[0]
    n_row, n_col = lax.axis_size("row"), lax.axis_size("col")
    rows, cols = mech // n_row, mech // n_col
    size = cav // n_row
    sets = enter(
        rho_real.reshape(-1, LANES), rho_imag.reshape(-1, LANES), cav_real, cav_imag, rows, cols
    )
    chunks = len(sets)

    place = lax.axis_index("row")
    member = lax.axis_index("col")
    far_half = place >= n_row // 2
    is_end = (place == 0) | (place == n_row - 1)
    flags = jnp.stack([far_half, is_end]).astype(jnp.int32)
    lanes = jnp.arange(chunks * LANES)
    uppers, _ = pair_tables(n_row)
    own_lanes = ((member >= len(uppers)) & ((lanes // size) == (lanes % size))).astype(jnp.int32)

    def order(matrix):
        shaped = matrix.reshape(n_row, rows, n_row, rows)
        return jnp.where(far_half, shaped[::-1, :, ::-1], shaped).reshape(mech, mech)

    mixer_real, mixer_imag = order(mech_real), order(mech_imag)
    outside = (jnp.arange(mech) >= rows)[None, :]
    away_real = jnp.where(outside, mixer_real[:rows], 0.0)
    away_imag = jnp.where(outside, mixer_imag[:rows], 0.0)
    whole = realified(
        jnp.concatenate([away_real, mixer_real[rows : 2 * rows]]),
        jnp.concatenate([away_imag, mixer_imag[rows : 2 * rows]]),
        1.0,
    )
    end_line = realified(mixer_real[:rows], mixer_imag[:rows], 1.0)
    bra = realified(mixer_real, mixer_imag, -1.0)
    own = [own_lanes[chunk * LANES : (chunk + 1) * LANES][None] for chunk in range(chunks)]

    state = {("set", chunk): sets[chunk] for chunk in range(chunks)}
    for tick in range(chunks + 5):
        fresh, moved, mixed, sent, last, gone = (tick - back for back in range(6))
        made = {}
        if fresh < chunks:
            made["row", fresh] = swap_plane(state.pop(("set", fresh)))
        if 0 <= gone < chunks:
            made["done", gone] = swap_plane(state.pop(("out", gone)))
        if 0 <= moved < chunks:
            end, ends, mids = pick_blocks(state["row", moved], flags)
            made["end", moved] = lax.ppermute(end, "row", INNER)
            made["ends", moved] = lax.ppermute(ends, "row", INNER)
            made["mids", moved] = lax.ppermute(mids, "row", CROSS)
        if 0 <= sent < chunks:
            made["partial", sent] = lax.ppermute(state.pop(("sent", sent)), "row", BACK)
        if 0 <= mixed < chunks:
            end, ends, mids = (state.pop((name, mixed)) for name in ("end", "ends", "mids"))
            corner = lax.ppermute(end, "row", CROSS)
            made["sent", mixed], made["mine", mixed] = mix_kets(
                state["row", mixed], end, ends, mids, corner, own[mixed], flags, whole
            )
        if 0 <= last < chunks:
            parts = [state.pop((name, last)) for name in ("row", "partial", "mine")]
            made["out", last] = mix_bras(*parts, own[last], flags, end_line, bra)
        state.update(made)
        if tick > chunks:
            continue
        names = sorted(state)
        state.update(zip(names, lax.optimization_barrier([state[name] for name in names])))
    results = [state["done", chunk] for chunk in range(chunks)]
    final = leave(results, cav, rows, cols)
    return final[0].reshape(block_shape), final[1].reshape(block_shape)


def fits(mesh, mech, cav):
    n_row, n_col = mesh.shape["row"], mesh.shape["col"]
    if n_row != 4 or n_col != 2 * n_row or mech % n_col:
        return False
    return kernels_fit(mech // n_row, mech // n_col, cav)


def solution(mesh):
    def whole(rho_real, rho_imag, cav_real, cav_imag, mech_real, mech_imag):
        local = fast_local if fits(mesh, mech_real.shape[0], cav_real.shape[0]) else general_local
        return jax.shard_map(
            local,
            mesh=mesh,
            in_specs=(P("row", "col", None), P("row", "col", None), P(), P(), P(), P()),
            out_specs=(P("row", "col", None), P("row", "col", None)),
            check_vma=False,
        )(rho_real, rho_imag, cav_real, cav_imag, mech_real, mech_imag)

    return whole
```
